128 devices in a mesh: seq: 16 (over x_hi, y, core), fsdp: 2 (over x_lo), dp: 4 (over z).
Axes of the slice: x: 4 (x_hi: 2, x_lo: 2; x = x_hi * 2 + x_lo), y: 4, z: 4, core: 2. Of those that a mesh axis runs over, the one named last changes fastest.
Arguments:
- queries: bfloat16 [8, 4096, 4096], P(('fsdp', 'dp'), 'seq'), may hold values from -160 to 160
- hidden: bfloat16 [8, 4096, 8192], P(('fsdp', 'dp'), 'seq'), may hold values from -8 to 8
- key_weight: bfloat16 [8192, 512], P('fsdp'), may hold values from -1 to 1
- doc_lengths: int32 [8, 32], P(('fsdp', 'dp')), may hold values from 1 to 256, 4096 in all within a row
- entropy_cot: bfloat16 [8, 4096, 32], P(('fsdp', 'dp'), 'seq'), may hold values from -600 to 600
Outputs:
- entropy: float32 [8, 4096, 32], P(('fsdp', 'dp'), 'seq')
- grad_queries: bfloat16 [8, 4096, 4096], P(('fsdp', 'dp'), 'seq')
- grad_key_weight: bfloat16 [8192, 512], P('fsdp')
The draws below stay inside these ranges and needn't reach their ends.
Inputs may be any that keep to these rules, and one draw needn't show every extreme that they name: `doc_lengths`: each sequence's 32 documents are packed in order, their lengths sum to 4096, and the longest is exactly 256.
All inputs are finite; a program needn't handle non-finite values.
Results may differ from the reference program's by a relative error of at most 0.0088.
Values may be sent and summed in bfloat16 or wider, within the bound.
No kernel may reach another device: no remote copies, remote signals or barrier semaphores. Data moves between devices by JAX's collectives and lax.ppermute only.
A program may use at most 128 MiB of HBM per device.

```python
import math
import jax
import jax.numpy as jnp
import numpy as np
from jax import lax

D = 8192
QH = 32
KVH = 4
HD = 128
LENGTH = 4096
DOC = 256
NDOC = 32
SEQS = 8


def weight_values(key):
    values = jax.random.normal(jax.random.fold_in(key, 202), (D, KVH * HD), jnp.float32) * D ** (-0.5)
    return jnp.clip(values, -1.0, 1.0)


def hidden_values(key):
    values = jax.random.normal(jax.random.fold_in(key, 101), (SEQS, LENGTH, D), jnp.float32)
    return jnp.clip(values, -8.0, 8.0)


def draw_hidden(key, part):
    return hidden_values(key).astype(jnp.bfloat16)


def draw_key_weight(key, part):
    return weight_values(key).astype(jnp.bfloat16)


def draw_queries(key, part):
    values = jnp.clip(jax.random.normal(jax.random.fold_in(key, 303), (SEQS, LENGTH, QH * HD), jnp.float32), -6.0, 6.0)
    return values.astype(jnp.bfloat16)


def shard_levels(rng, extent, shards, least, high):
    gain, own = 1.0, jax.random.fold_in(rng, 6)
    for dim, parts in shards:
        draws = jnp.exp(jax.random.uniform(jax.random.fold_in(own, dim), (parts,), jnp.float32, least / len(shards), high / len(shards)))
        gain = gain * jnp.repeat(draws, extent[dim] // parts).reshape([-1 if axis == dim else 1 for axis in range(len(extent))])
    return gain


def split_up(number_of, total, most, lean):
    weights = [(1 << 20) // math.isqrt(standing ** lean) + 1 for standing in range(2, number_of + 1)]
    rest, holding = total - most - (number_of - 1), [1] * (number_of - 1)
    while rest > 0:
        free = [i for i in range(number_of - 1) if holding[i] < most]
        pool, remaining = sum([weights[i] for i in free]), rest
        for i in free:
            more = min(most - holding[i], max(1, remaining * weights[i] // pool), rest)
            holding[i] = holding[i] + more
            rest = rest - more
    return np.array([most] + holding)


def ragged(key, amount, total, reach, skew):
    if amount == 2:
        one = jax.random.randint(key, (), max(1, total - reach), min(reach, total - 1) + 1)
        return jnp.stack([one, total - one])
    sizes = jnp.asarray(split_up(amount, total, reach, skew), jnp.int32)
    pairs = (amount - 1) // 2
    donor, sink = sizes[1:1 + 2 * pairs:2], sizes[2:2 + 2 * pairs:2]
    margin = jnp.minimum(donor - 1, reach - sink)
    passed = jax.random.randint(jax.random.fold_in(key, 1), (pairs,), 0, 1 << 20) % (margin + 1)
    sizes = sizes.at[1:1 + 2 * pairs:2].set(donor - passed).at[2:2 + 2 * pairs:2].set(sink + passed)
    return sizes[jax.random.permutation(jax.random.fold_in(key, 2), amount)]


def normal_values(stream_key, extent, width, most, shards=(), kind=jnp.bfloat16):
    values = width * jax.random.normal(stream_key, extent, jnp.float32)
    if shards:
        values = values * shard_levels(stream_key, extent, shards, -0.22, 0.18)
    return jnp.clip(values, -most, most).astype(kind)


def setup_inputs(seed: int = 0) -> dict:
    keys = jax.random.split(jax.random.key(seed), 6)
    queries = draw_queries(jax.random.fold_in(keys[5], 71), 0)
    hidden = draw_hidden(jax.random.fold_in(keys[5], 71), 0)
    key_weight = draw_key_weight(jax.random.fold_in(keys[5], 71), 0)
    doc_lengths = jax.vmap(lambda own: ragged(own, NDOC, LENGTH, DOC, 1))(jax.random.split(keys[3], SEQS)).reshape((SEQS, NDOC)).astype(jnp.int32)
    entropy_cot = normal_values(keys[4], (SEQS, LENGTH, QH), 100.0, 600.0, ((0, 8), (1, 16)))
    return {"queries": queries, "hidden": hidden, "key_weight": key_weight, "doc_lengths": doc_lengths, "entropy_cot": entropy_cot}


def document_index(lengths, seq_len):
    ends = jnp.cumsum(lengths.astype(jnp.int32)).astype(jnp.int32)
    position = jnp.arange(seq_len, dtype=jnp.int32)
    return jnp.sum((ends[None, :] <= position[:, None]).astype(jnp.int32), axis=1).astype(jnp.int32)


def attend(queries, key_rows, cotangent, doc_index, anchor, doc_len):
    row_count, key_heads, group_size, head_size = queries.shape
    full_len = key_rows.shape[0]
    block_rows = min(512, row_count)
    window = block_rows + doc_len
    factor = head_size ** -0.5
    keys_padded = jnp.concatenate([jnp.zeros((doc_len, key_heads, head_size), key_rows.dtype), key_rows], axis=0)
    index_padded = jnp.concatenate([jnp.full((doc_len,), -1, jnp.int32), doc_index.astype(jnp.int32)], axis=0)

    def one_block(step_index, state_now):
        entropy, grad_query, grad_key = state_now
        row_start = (step_index * block_rows).astype(jnp.int32)
        position = (anchor + row_start).astype(jnp.int32)
        query_block = lax.dynamic_slice_in_dim(queries, row_start, block_rows, 0).astype(jnp.float32)
        weight_block = lax.dynamic_slice_in_dim(cotangent, row_start, block_rows, 0).astype(jnp.float32)
        key_block = lax.dynamic_slice_in_dim(keys_padded, position, window, 0).astype(jnp.float32)
        key_docs = lax.dynamic_slice_in_dim(index_padded, position, window, 0)
        query_docs = lax.dynamic_slice_in_dim(doc_index.astype(jnp.int32), position, block_rows, 0)
        query_pos = position + jnp.arange(block_rows, dtype=jnp.int32)
        key_pos = position - doc_len + jnp.arange(window, dtype=jnp.int32)
        visible = (query_docs[:, None] == key_docs[None, :]) & (key_pos[None, :] <= query_pos[:, None])
        scores = jnp.einsum("rkgd,wkd->kgrw", query_block, key_block, precision=lax.Precision.HIGHEST) * factor
        scores = jnp.where(visible, scores, -1e30)
        row_max = jnp.max(scores, axis=-1, keepdims=True)
        powers = jnp.exp(scores - row_max)
        denominator = jnp.sum(powers, axis=-1, keepdims=True)
        probability = powers / denominator
        mean_score = jnp.sum(jnp.where(visible, probability * scores, 0.0), axis=-1, keepdims=True)
        block_entropy = (row_max + jnp.log(denominator) - mean_score)[..., 0]
        row_weight = jnp.transpose(weight_block, (1, 2, 0))[..., None]
        slope = jnp.where(visible, row_weight * probability * (mean_score - scores), 0.0).astype(jnp.bfloat16)
        slope = lax.optimization_barrier(slope).astype(jnp.float32)
        query_part = jnp.einsum("kgrw,wkd->rkgd", slope, key_block, precision=lax.Precision.HIGHEST) * factor
        key_part = jnp.einsum("kgrw,rkgd->wkd", slope, query_block, precision=lax.Precision.HIGHEST) * factor
        entropy = lax.dynamic_update_slice_in_dim(entropy, jnp.transpose(block_entropy, (2, 0, 1)), row_start, 0)
        grad_query = lax.dynamic_update_slice_in_dim(grad_query, query_part, row_start, 0)
        previous = lax.dynamic_slice_in_dim(grad_key, position, window, 0)
        grad_key = lax.dynamic_update_slice_in_dim(grad_key, previous + key_part, position, 0)
        return entropy, grad_query, grad_key

    initial = (jnp.zeros((row_count, key_heads, group_size), jnp.float32),
               jnp.zeros((row_count, key_heads, group_size, head_size), jnp.float32),
               jnp.zeros((full_len + doc_len, key_heads, head_size), jnp.float32))
    entropy, grad_query, grad_key = lax.fori_loop(0, row_count // block_rows, one_block, initial)
    return entropy, grad_query, grad_key[doc_len:]


def reference(queries, hidden, key_weight, doc_lengths, entropy_cot):
    group_size = QH // KVH

    def one_sequence(items):
        query_rows, hidden_rows, lengths, cot_rows = items
        doc_index = document_index(lengths, LENGTH)
        key_rows = jnp.dot(hidden_rows, key_weight, preferred_element_type=jnp.float32).astype(jnp.bfloat16)
        key_rows = key_rows.reshape(LENGTH, KVH, HD)
        query_four = query_rows.reshape(LENGTH, KVH, group_size, HD)
        cot_three = cot_rows.reshape(LENGTH, KVH, group_size)
        outcome = [attend(query_four[:, head_index:head_index + 1], key_rows[:, head_index:head_index + 1],
                          cot_three[:, head_index:head_index + 1], doc_index, 0, DOC) for head_index in range(KVH)]
        entropy = jnp.concatenate([item_set[0] for item_set in outcome], axis=1).reshape(LENGTH, QH)
        grad_query = jnp.concatenate([item_set[1] for item_set in outcome], axis=1).reshape(LENGTH, QH * HD)
        key_grad = jnp.concatenate([item_set[2] for item_set in outcome], axis=1).reshape(LENGTH, KVH * HD)
        key_grad = key_grad.astype(jnp.bfloat16)
        weight_grad = jnp.dot(hidden_rows.T, key_grad, preferred_element_type=jnp.float32)
        return entropy, grad_query.astype(jnp.bfloat16), weight_grad

    entropy, grad_query, weight_grads = lax.map(one_sequence, (queries, hidden, doc_lengths, entropy_cot))
    weight_grad = jnp.sum(weight_grads, axis=0) * ((SEQS * LENGTH) ** -0.5)
    return entropy, grad_query, weight_grad.astype(jnp.bfloat16)
```

```python
import functools
import math

import jax
import jax.numpy as jnp
from jax import lax
from jax.experimental import pallas as pl
from jax.experimental.pallas import tpu as pltpu
from jax.sharding import PartitionSpec as P

QH = 32
KVH = 4
HD = 128
GROUP = QH // KVH
BF = jnp.bfloat16
F32 = jnp.float32
AXES = ("seq", "fsdp", "dp")
FACTOR = HD ** (-0.5)
EXP_SCALE = FACTOR * math.log2(math.e)
NEG = -1e30


def coords(index):
    seq, rest = divmod(index, 8)
    fsdp, z = divmod(rest, 4)
    return seq // 8, (seq // 2) % 4, seq % 2, fsdp, z


def linear(xh, y, core, xl, z):
    return ((xh * 8 + y * 2 + core) * 2 + xl) * 4 + z


def move(value, where):
    pairs = []
    for index in range(128):
        target = where(*coords(index))
        if target is not None:
            pairs.append((index, linear(*target)))
    return lax.ppermute(value, AXES, pairs)


def along_x(xh, y, core, xl, z, step, other=0):
    x = (xh * 2 + xl + step) % 4
    return x // 2, y, core ^ other, x % 2, z


def params(**kw):
    return pltpu.CompilerParams(vmem_limit_bytes=56 << 20, **kw)


def cost(flops, moved):
    return pl.CostEstimate(flops=int(flops), bytes_accessed=int(moved), transcendentals=0)


def own_half_kernel(place, hidden, weight, out):
    @pl.when(pl.program_id(0) == 0)
    def _():
        out[...] = jnp.zeros_like(out)

    out[...] += jnp.dot(hidden[...], weight[...], preferred_element_type=F32)


def project_own(place, tokens, weight):
    rows, model = tokens.shape
    half, width = weight.shape
    step = half // 4
    return pl.pallas_call(
        own_half_kernel,
        grid_spec=pltpu.PrefetchScalarGridSpec(
            num_scalar_prefetch=1,
            grid=(4,),
            in_specs=[
                pl.BlockSpec((rows, step), lambda i, p: (0, p[0] * 4 + i)),
                pl.BlockSpec((step, width), lambda i, p: (i, 0)),
            ],
            out_specs=pl.BlockSpec((rows, width), lambda i, p: (0, 0)),
        ),
        out_shape=jax.ShapeDtypeStruct((rows, width), F32),
        compiler_params=params(),
        cost_estimate=cost(2 * rows * half * width, 6 << 20),
        name="project_own",
    )(place, tokens, weight)


def pair_kernel(place, hidden_a, hidden_b, weight_a, weight_b, total, out):
    acc = total[...] + jnp.dot(hidden_a[...], weight_a[...], preferred_element_type=F32)
    acc = acc + jnp.dot(hidden_b[...], weight_b[...], preferred_element_type=F32)
    out[...] = acc.astype(out.dtype)


def project_pair(place, tokens, weight_a, weight_b, total, chunk, dtype):
    rows, model = tokens.shape
    step, width = weight_a.shape

    def block_a(i, p):
        return (0, (1 - p[0]) * 4 + p[1] * 2 + chunk)

    def block_b(i, p):
        return (0, (1 - p[0]) * 4 + (1 - p[1]) * 2 + chunk)

    whole = lambda i, p: (0, 0)
    return pl.pallas_call(
        pair_kernel,
        grid_spec=pltpu.PrefetchScalarGridSpec(
            num_scalar_prefetch=1,
            grid=(1,),
            in_specs=[
                pl.BlockSpec((rows, step), block_a),
                pl.BlockSpec((rows, step), block_b),
                pl.BlockSpec((step, width), whole),
                pl.BlockSpec((step, width), whole),
                pl.BlockSpec((rows, width), whole),
            ],
            out_specs=pl.BlockSpec((rows, width), whole),
        ),
        out_shape=jax.ShapeDtypeStruct((rows, width), dtype),
        compiler_params=params(),
        cost_estimate=cost(4 * rows * step * width, 4 << 20),
        name="project_pair",
    )(place, tokens, tokens, weight_a, weight_b, total)


def attend_kernel(place, lengths, query, key_own, key_halo, weight, entropy, grad_query, grad_own,
                  grad_halo, bias, keys, keys_t):
    @pl.when(pl.program_id(0) == 0)
    def _():
        base = place[2] * 256
        position = base + lax.broadcasted_iota(jnp.int32, (8, 256), 1)

        def add(i, state):
            end, first = state
            end = end + lengths[0, i]
            return end, jnp.where(position >= end, end, first)

        _, first = lax.fori_loop(
            0, lengths.shape[1], add, (jnp.int32(0), jnp.zeros((8, 256), jnp.int32))
        )
        for half in range(2):
            begin = first[0:1, half * 128:(half + 1) * 128]
            here = position[0:1, half * 128:(half + 1) * 128]
            there = base - 256 + half * 128 + lax.broadcasted_iota(jnp.int32, (384, 128), 0)
            seen = (there >= begin) & (there <= here)
            value = jnp.where(seen, 0.0, NEG)
            bias[half, :, 0:128] = value
            bias[half, :, 128:256] = value

    keys[0:256, :] = key_halo[...]
    keys[256:512, :] = key_own[...]
    keys_t[...] = keys[...].T
    weights = weight[...].astype(F32)
    sums = [None, None]
    for pair in range(GROUP // 2):
        cols = [slice((2 * pair + k) * HD, (2 * pair + k + 1) * HD) for k in range(2)]
        for half in range(2):
            rows = slice(half * 128, (half + 1) * 128)
            window = slice(half * 128, half * 128 + 384)
            stack = jnp.concatenate([query[rows, cols[0]], query[rows, cols[1]]], axis=0)
            raw = lax.dot_general(
                keys[window, :], stack, (((1,), (1,)), ((), ())), preferred_element_type=F32
            ) + bias[half]
            top = jnp.max(raw, axis=0, keepdims=True)
            gap = raw - top
            power = jnp.exp2(gap * EXP_SCALE)
            den = jnp.sum(power, axis=0, keepdims=True)
            mean = jnp.sum(power * gap, axis=0, keepdims=True) / den
            row_weight = jnp.concatenate(
                [weights[2 * pair:2 * pair + 1, rows], weights[2 * pair + 1:2 * pair + 2, rows]], axis=1
            )
            slope_b = row_weight * FACTOR / den
            slope_a = slope_b * mean
            slope = (power * (slope_a - slope_b * gap)).astype(BF)
            level = jnp.log(den) - FACTOR * mean
            entropy[2 * pair:2 * pair + 1, rows] = level[:, 0:128]
            entropy[2 * pair + 1:2 * pair + 2, rows] = level[:, 128:256]
            turned = jnp.dot(keys_t[:, window], slope, preferred_element_type=F32) * FACTOR
            straight = turned.T.astype(BF)
            grad_query[rows, cols[0]] = straight[0:128]
            grad_query[rows, cols[1]] = straight[128:256]
            part = jnp.dot(slope, stack, preferred_element_type=F32)
            sums[half] = part if sums[half] is None else sums[half] + part
    low, high = sums
    grad_halo[0:128, :] = (low[0:128] * FACTOR).astype(grad_halo.dtype)
    grad_halo[128:256, :] = ((low[128:256] + high[0:128]) * FACTOR).astype(grad_halo.dtype)
    grad_own[0:128, :] = (low[256:384] + high[128:256]) * FACTOR
    grad_own[128:256, :] = high[256:384] * FACTOR


def attend(place, lengths, queries, key_own, key_halo, weight):
    rows, width = queries.shape
    wide = GROUP * HD
    by_head = lambda j, p, l: (0, j)
    return pl.pallas_call(
        attend_kernel,
        grid_spec=pltpu.PrefetchScalarGridSpec(
            num_scalar_prefetch=2,
            grid=(KVH,),
            in_specs=[
                pl.BlockSpec((rows, wide), by_head),
                pl.BlockSpec((rows, HD), by_head),
                pl.BlockSpec((rows, HD), by_head),
                pl.BlockSpec((GROUP, rows), lambda j, p, l: (j, 0)),
            ],
            out_specs=[
                pl.BlockSpec((GROUP, rows), lambda j, p, l: (j, 0)),
                pl.BlockSpec((rows, wide), by_head),
                pl.BlockSpec((rows, HD), by_head),
                pl.BlockSpec((rows, HD), by_head),
            ],
            scratch_shapes=[
                pltpu.VMEM((2, 384, 256), F32),
                pltpu.VMEM((512, HD), BF),
                pltpu.VMEM((HD, 512), BF),
            ],
        ),
        out_shape=[
            jax.ShapeDtypeStruct((QH, rows), F32),
            jax.ShapeDtypeStruct((rows, width), BF),
            jax.ShapeDtypeStruct((rows, KVH * HD), F32),
            jax.ShapeDtypeStruct((rows, KVH * HD), BF),
        ],
        compiler_params=params(),
        cost_estimate=cost(4 << 30, 6 << 20),
        name="attend",
    )(place, lengths, queries, key_own, key_halo, weight)


def weight_grad_kernel(place, *refs):
    hidden, grads, outs = refs[0:6], refs[6:12], refs[12:]
    total = None
    for piece, grad in zip(hidden, grads):
        part = lax.dot_general(
            piece[...], grad[...], (((0,), (0,)), ((), ())), preferred_element_type=F32
        )
        total = part if total is None else total + part
    low = total.astype(BF)
    for k in range(8):

        @pl.when(pl.program_id(0) == k)
        def _():
            outs[k][...] = low


def weight_grad(place, tokens, pieces, grads):
    def chunk(i, p):
        own = jnp.where(i < 4, p[3], p[4])
        return jnp.where(i < 4, 0, 4) + (own + i) % 4

    def own_block(i, p):
        return (0, (p[0] * 2 + p[1]) * 8 + chunk(i, p))

    whole = lambda i, p: (0, 0)
    return pl.pallas_call(
        weight_grad_kernel,
        grid_spec=pltpu.PrefetchScalarGridSpec(
            num_scalar_prefetch=1,
            grid=(8,),
            in_specs=[pl.BlockSpec((256, 256), own_block)]
            + [pl.BlockSpec((v.shape[0], 256), lambda i, p: (0, chunk(i, p))) for v in pieces]
            + [pl.BlockSpec(v.shape, whole) for v in grads],
            out_specs=[pl.BlockSpec((256, 512), whole)] * 8,
        ),
        out_shape=[jax.ShapeDtypeStruct((256, 512), BF)] * 8,
        compiler_params=params(),
        cost_estimate=cost(2 * 1024 * 2048 * 512, 8 << 20),
        name="weight_grad",
    )(place, tokens, *pieces, *grads)


def sum_split_kernel(place, *refs):
    first, second, outs = refs[0:4], refs[4:8], refs[8:16]
    work = refs[16]
    for half, group in enumerate((first, second)):
        total = group[0][...].astype(F32)
        for ref in group[1:]:
            total = total + ref[...].astype(F32)
        work[half] = total
    for half in range(2):
        own = place[4] if half == 0 else place[3]
        for d in range(4):
            start = pl.multiple_of(((own + d) % 4) * 64, 64)
            outs[4 * half + d][...] = work[half, pl.ds(start, 64), :].astype(BF)


def sum_split(place, first, second):
    return pl.pallas_call(
        sum_split_kernel,
        in_specs=[pl.BlockSpec(memory_space=pltpu.SMEM)] + [pl.BlockSpec(memory_space=pltpu.VMEM)] * 8,
        out_specs=[pl.BlockSpec(memory_space=pltpu.VMEM)] * 8,
        out_shape=[jax.ShapeDtypeStruct((64, 512), BF)] * 8,
        scratch_shapes=[pltpu.VMEM((2, 256, 512), F32)],
        compiler_params=params(),
        cost_estimate=cost(2 << 20, 3 << 20),
        name="sum_split",
    )(place, *first, *second)


def sum_join_kernel(*refs):
    first, second, out = refs[0:4], refs[4:8], refs[8]
    for half, group in enumerate((first, second)):
        total = group[0][...].astype(F32)
        for ref in group[1:]:
            total = total + ref[...].astype(F32)
        out[half * 64:(half + 1) * 64, :] = total.astype(BF)


def sum_join(first, second):
    return pl.pallas_call(
        sum_join_kernel,
        in_specs=[pl.BlockSpec(memory_space=pltpu.VMEM)] * 8,
        out_specs=pl.BlockSpec(memory_space=pltpu.VMEM),
        out_shape=jax.ShapeDtypeStruct((128, 512), BF),
        compiler_params=params(),
        cost_estimate=cost(1 << 20, 1 << 20),
        name="sum_join",
    )(*first, *second)


def finish_kernel(scale, mine, other, first, second):
    total = (mine[...].astype(F32) + other[...].astype(F32)) * scale
    low = total.astype(BF)
    first[...] = low[0:64]
    second[...] = low[64:128]


def finish(mine, other, scale):
    return pl.pallas_call(
        functools.partial(finish_kernel, scale),
        in_specs=[pl.BlockSpec(memory_space=pltpu.VMEM)] * 2,
        out_specs=[pl.BlockSpec(memory_space=pltpu.VMEM)] * 2,
        out_shape=[jax.ShapeDtypeStruct((64, 512), BF)] * 2,
        compiler_params=params(),
        cost_estimate=cost(1 << 20, 1 << 20),
        name="finish",
    )(mine, other)


def gather_small_kernel(place, *refs):
    first, second, outs = refs[0:4], refs[4:8], refs[8:10]
    for half, group in enumerate((first, second)):
        own = place[4] if half == 0 else place[3]
        for d in range(4):
            start = pl.multiple_of(((own + 4 - d) % 4) * 64, 64)
            outs[half][pl.ds(start, 64), :] = group[d][...]


def gather_small(place, first, second):
    return pl.pallas_call(
        gather_small_kernel,
        in_specs=[pl.BlockSpec(memory_space=pltpu.SMEM)] + [pl.BlockSpec(memory_space=pltpu.VMEM)] * 8,
        out_specs=[pl.BlockSpec(memory_space=pltpu.VMEM)] * 2,
        out_shape=[jax.ShapeDtypeStruct((256, 512), BF)] * 2,
        compiler_params=params(),
        cost_estimate=cost(1 << 20, 1 << 20),
        name="gather_small",
    )(place, *first, *second)


def gather_large_kernel(place, *refs):
    out = refs[16]
    for side in range(2):
        core = place[1] if side == 0 else 1 - place[1]
        for half in range(2):
            own = place[3] if half == 0 else place[4]
            for d in range(4):
                start = core * 2048 + half * 1024 + ((own + 4 - d) % 4) * 256
                start = pl.multiple_of(start, 256)
                out[pl.ds(start, 256), :] = refs[8 * side + 4 * half + d][...]


def gather_large(place, mine, others):
    return pl.pallas_call(
        gather_large_kernel,
        in_specs=[pl.BlockSpec(memory_space=pltpu.SMEM)] + [pl.BlockSpec(memory_space=pltpu.VMEM)] * 16,
        out_specs=pl.BlockSpec(memory_space=pltpu.VMEM),
        out_shape=jax.ShapeDtypeStruct((4096, 512), BF),
        compiler_params=params(),
        cost_estimate=cost(1 << 20, 8 << 20),
        name="gather_large",
    )(place, *mine, *others)


def shift_y(d):
    return lambda xh, y, core, xl, z: (xh, (y + d) % 4, core, xl, z)


def shift_z(d):
    return lambda xh, y, core, xl, z: (xh, y, core, xl, (z + d) % 4)


def swap_core(xh, y, core, xl, z):
    return xh, y, 1 - core, xl, z


def next_rows(step):
    def where(xh, y, core, xl, z):
        seq = xh * 8 + y * 2 + core + step
        if seq < 0 or seq > 15:
            return None
        return seq // 8, (seq // 2) % 4, seq % 2, xl, z

    return where


def shards(queries, hidden, key_weight, doc_lengths, entropy_cot):
    tokens = hidden[0]
    rows, model = tokens.shape
    half, width = key_weight.shape
    seq, fsdp, z = lax.axis_index("seq"), lax.axis_index("fsdp"), lax.axis_index("dp")
    core, y = seq % 2, (seq // 2) % 4
    place = jnp.stack([fsdp, core, seq, y, z]).astype(jnp.int32)

    mine = lax.dynamic_slice_in_dim(key_weight, core * (half // 2), half // 2, 0)
    fetch = lambda xh, y, core, xl, z: along_x(xh, y, core, xl, z, 1 - 2 * core)
    got = [move(mine[k * half // 4:(k + 1) * half // 4], fetch) for k in range(2)]
    swapped = [move(v, swap_core) for v in got]
    total = project_own(place, tokens, key_weight)
    total = project_pair(place, tokens, got[0], swapped[0], total, 0, F32)
    key_own = project_pair(place, tokens, got[1], swapped[1], total, 1, BF)
    key_halo = move(key_own, next_rows(1))

    quarter = model // 4
    tied, _ = lax.optimization_barrier((tokens, got[1]))

    def column(first, last, is_fsdp, is_core):
        start = (is_fsdp * 2 + is_core) * quarter
        return lax.dynamic_slice(tied, (first, start), (last - first, quarter))

    split = rows // 2
    routes = [swap_core]
    for step in (1, -1):
        for other in (0, 1):
            routes.append(functools.partial(along_x, step=step, other=other))
    pieces = [move(column(0, rows, fsdp, 1 - core), routes[0])]
    for k, route in enumerate(routes[1:]):
        first = 0 if k < 2 else split
        pieces.append(
            move(column(first, first + split, 1 - fsdp, core if k % 2 == 0 else 1 - core), route)
        )

    entropy, grad_query, grad_own, grad_halo = attend(
        place, doc_lengths, queries[0], key_own, key_halo, entropy_cot[0].T
    )

    from_next = move(grad_halo, next_rows(-1))
    key_grad = (grad_own + from_next.astype(F32)).astype(BF)
    grads = [key_grad, move(key_grad, routes[0])]
    for k, route in enumerate(routes[1:]):
        first = 0 if k < 2 else split
        grads.append(move(key_grad[first:first + split], route))

    parts = weight_grad(place, tokens, pieces, grads)
    first = [parts[0]] + [move(parts[d], shift_y(d)) for d in (1, 2, 3)]
    second = [parts[4]] + [move(parts[4 + d], shift_z(d)) for d in (1, 2, 3)]
    parts = sum_split(place, first, second)
    first = [parts[0]] + [move(parts[d], shift_z(d)) for d in (1, 2, 3)]
    second = [parts[4]] + [move(parts[4 + d], shift_y(d)) for d in (1, 2, 3)]
    joined = sum_join(first, second)
    across = move(joined, lambda xh, y, core, xl, z: (1 - xh, y, core, xl, z))
    scale = (rows * 16 * 8) ** (-0.5)
    low, high = finish(joined, across, scale)
    first = [low] + [move(low, shift_z(d)) for d in (1, 2, 3)]
    second = [high] + [move(high, shift_y(d)) for d in (1, 2, 3)]
    low, high = gather_small(place, first, second)
    final = [low] + [move(low, shift_y(d)) for d in (1, 2, 3)]
    final += [high] + [move(high, shift_z(d)) for d in (1, 2, 3)]
    others = [move(v, swap_core) for v in final]
    grad_weight = gather_large(place, final, others)
    return entropy.T[None], grad_query[None], grad_weight


def solution(mesh):
    return jax.shard_map(
        shards,
        mesh=mesh,
        in_specs=(
            P(("fsdp", "dp"), "seq", None),
            P(("fsdp", "dp"), "seq", None),
            P("fsdp", None),
            P(("fsdp", "dp"), None),
            P(("fsdp", "dp"), "seq", None),
        ),
        out_specs=(P(("fsdp", "dp"), "seq", None), P(("fsdp", "dp"), "seq", None), P("fsdp", None)),
        check_vma=False,
    )
```

```python
import functools
import math

import jax
import jax.numpy as jnp
from jax import lax
from jax.experimental import pallas as pl
from jax.experimental.pallas import tpu as pltpu
from jax.sharding import Mesh, PartitionSpec as P

QH = 32
KVH = 4
HD = 128
GROUP = QH // KVH
BF = jnp.bfloat16
F32 = jnp.float32
AXES = ("xh", "y", "core", "xl", "z")
FACTOR = HD ** (-0.5)
EXP_SCALE = FACTOR * math.log2(math.e)
NEG = -1e30


def coords(index):
    seq, rest = divmod(index, 8)
    fsdp, z = divmod(rest, 4)
    return seq // 8, (seq // 2) % 4, seq % 2, fsdp, z


def linear(xh, y, core, xl, z):
    return ((xh * 8 + y * 2 + core) * 2 + xl) * 4 + z


def move(value, where):
    pairs = []
    for index in range(128):
        target = where(*coords(index))
        if target is not None:
            pairs.append((index, linear(*target)))
    return lax.ppermute(value, AXES, pairs)


def along_x(xh, y, core, xl, z, step, other=0):
    x = (xh * 2 + xl + step) % 4
    return x // 2, y, core ^ other, x % 2, z


def params(mib):
    return pltpu.CompilerParams(vmem_limit_bytes=mib << 20)


def cost(flops, moved):
    return pl.CostEstimate(flops=int(flops), bytes_accessed=int(moved), transcendentals=0)


def own_half_kernel(place, hidden, weight, out):
    @pl.when(pl.program_id(0) == 0)
    def _():
        out[...] = jnp.zeros_like(out)

    out[...] += jnp.dot(hidden[...], weight[...], preferred_element_type=F32)


def project_own(place, tokens, weight):
    rows, model = tokens.shape
    half, width = weight.shape
    step = half // 4
    return pl.pallas_call(
        own_half_kernel,
        grid_spec=pltpu.PrefetchScalarGridSpec(
            num_scalar_prefetch=1,
            grid=(4,),
            in_specs=[
                pl.BlockSpec((rows, step), lambda i, p: (0, p[0] * 4 + i)),
                pl.BlockSpec((step, width), lambda i, p: (i, 0)),
            ],
            out_specs=pl.BlockSpec((rows, width), lambda i, p: (0, 0)),
        ),
        out_shape=jax.ShapeDtypeStruct((rows, width), F32),
        compiler_params=params(8),
        cost_estimate=cost(2 * rows * half * width, 6 << 20),
        name="project_own",
    )(place, tokens, weight)


def add_kernel(count, place, *refs):
    hidden, weights, total, out = refs[:count], refs[count:2 * count], refs[2 * count], refs[2 * count + 1]
    acc = total[...]
    for h, w in zip(hidden, weights):
        acc = acc + jnp.dot(h[...], w[...], preferred_element_type=F32)
    out[...] = acc.astype(out.dtype)


def project_add(place, tokens, weights, which, total, dtype):
    rows, model = tokens.shape
    step, width = weights[0].shape

    def block(other, chunk):
        def index(i, p):
            return (0, (1 - p[0]) * 4 + ((1 - p[1]) if other else p[1]) * 2 + chunk)

        return index

    whole = lambda i, p: (0, 0)
    return pl.pallas_call(
        functools.partial(add_kernel, len(weights)),
        grid_spec=pltpu.PrefetchScalarGridSpec(
            num_scalar_prefetch=1,
            grid=(1,),
            in_specs=[pl.BlockSpec((rows, step), block(*w)) for w in which]
            + [pl.BlockSpec((step, width), whole) for _ in which]
            + [pl.BlockSpec((rows, width), whole)],
            out_specs=pl.BlockSpec((rows, width), whole),
        ),
        out_shape=jax.ShapeDtypeStruct((rows, width), dtype),
        compiler_params=params(12),
        cost_estimate=cost(2 * len(weights) * rows * step * width, 2 << 20),
        name="project_add",
    )(place, *([tokens] * len(weights)), *weights, total)


def attend_kernel(place, lengths, query, key_own, key_halo, weight, entropy, grad_query, grad_own,
                  grad_halo, bias, keys, keys_t):
    @pl.when(pl.program_id(0) == 0)
    def _():
        base = place[2] * 256
        position = base + lax.broadcasted_iota(jnp.int32, (8, 256), 1)

        def add(i, state):
            end, first = state
            end = end + lengths[0, i]
            return end, jnp.where(position >= end, end, first)

        _, first = lax.fori_loop(
            0, lengths.shape[1], add, (jnp.int32(0), jnp.zeros((8, 256), jnp.int32))
        )
        for half in range(2):
            begin = first[0:1, half * 128:(half + 1) * 128]
            here = position[0:1, half * 128:(half + 1) * 128]
            there = base - 256 + half * 128 + lax.broadcasted_iota(jnp.int32, (384, 128), 0)
            seen = (there >= begin) & (there <= here)
            value = jnp.where(seen, 0.0, NEG)
            bias[half, :, 0:128] = value
            bias[half, :, 128:256] = value

    keys[0:256, :] = key_halo[...]
    keys[256:512, :] = key_own[...]
    keys_t[...] = keys[...].T
    weights = weight[...].astype(F32)
    sums = [None, None]
    for pair in range(GROUP // 2):
        cols = [slice((2 * pair + k) * HD, (2 * pair + k + 1) * HD) for k in range(2)]
        for half in range(2):
            rows = slice(half * 128, (half + 1) * 128)
            window = slice(half * 128, half * 128 + 384)
            stack = jnp.concatenate([query[rows, cols[0]], query[rows, cols[1]]], axis=0)
            raw = lax.dot_general(
                keys[window, :], stack, (((1,), (1,)), ((), ())), preferred_element_type=F32
            ) + bias[half]
            top = jnp.max(raw, axis=0, keepdims=True)
            gap = raw - top
            power = jnp.exp2(gap * EXP_SCALE)
            den = jnp.sum(power, axis=0, keepdims=True)
            mean = jnp.sum(power * gap, axis=0, keepdims=True) / den
            row_weight = jnp.concatenate(
                [weights[2 * pair:2 * pair + 1, rows], weights[2 * pair + 1:2 * pair + 2, rows]], axis=1
            )
            slope_b = row_weight * FACTOR / den
            slope_a = slope_b * mean
            slope = (power * (slope_a - slope_b * gap)).astype(BF)
            level = jnp.log(den) - FACTOR * mean
            entropy[2 * pair:2 * pair + 1, rows] = level[:, 0:128]
            entropy[2 * pair + 1:2 * pair + 2, rows] = level[:, 128:256]
            turned = jnp.dot(keys_t[:, window], slope, preferred_element_type=F32) * FACTOR
            straight = turned.T.astype(BF)
            grad_query[rows, cols[0]] = straight[0:128]
            grad_query[rows, cols[1]] = straight[128:256]
            part = jnp.dot(slope, stack, preferred_element_type=F32)
            sums[half] = part if sums[half] is None else sums[half] + part
    low, high = sums
    grad_halo[0:128, :] = (low[0:128] * FACTOR).astype(grad_halo.dtype)
    grad_halo[128:256, :] = ((low[128:256] + high[0:128]) * FACTOR).astype(grad_halo.dtype)
    grad_own[0:128, :] = (low[256:384] + high[128:256]) * FACTOR
    grad_own[128:256, :] = high[256:384] * FACTOR


def attend(place, lengths, queries, key_own, key_halo, weight):
    rows, width = queries.shape
    wide = GROUP * HD
    by_head = lambda j, p, l: (0, j)
    return pl.pallas_call(
        attend_kernel,
        grid_spec=pltpu.PrefetchScalarGridSpec(
            num_scalar_prefetch=2,
            grid=(KVH,),
            in_specs=[
                pl.BlockSpec((rows, wide), by_head),
                pl.BlockSpec((rows, HD), by_head),
                pl.BlockSpec((rows, HD), by_head),
                pl.BlockSpec((GROUP, rows), lambda j, p, l: (j, 0)),
            ],
            out_specs=[
                pl.BlockSpec((GROUP, rows), lambda j, p, l: (j, 0)),
                pl.BlockSpec((rows, wide), by_head),
                pl.BlockSpec((rows, HD), by_head),
                pl.BlockSpec((rows, HD), by_head),
            ],
            scratch_shapes=[
                pltpu.VMEM((2, 384, 256), F32),
                pltpu.VMEM((512, HD), BF),
                pltpu.VMEM((HD, 512), BF),
            ],
        ),
        out_shape=[
            jax.ShapeDtypeStruct((QH, rows), F32),
            jax.ShapeDtypeStruct((rows, width), BF),
            jax.ShapeDtypeStruct((rows, KVH * HD), F32),
            jax.ShapeDtypeStruct((rows, KVH * HD), BF),
        ],
        compiler_params=params(16),
        cost_estimate=cost(4 << 30, 6 << 20),
        name="attend",
    )(place, lengths, queries, key_own, key_halo, weight)


def weight_grad_kernel(place, *refs):
    hidden, grads, out = refs[0:6], refs[6:12], refs[12]
    total = None
    for piece, grad in zip(hidden, grads):
        part = lax.dot_general(
            piece[...], grad[...], (((0,), (0,)), ((), ())), preferred_element_type=F32
        )
        total = part if total is None else total + part
    out[...] = total.astype(BF)


def weight_grad(place, tokens, pieces, grads):
    whole = lambda i, p: (0, 0)
    return pl.pallas_call(
        weight_grad_kernel,
        grid_spec=pltpu.PrefetchScalarGridSpec(
            num_scalar_prefetch=1,
            grid=(8,),
            in_specs=[pl.BlockSpec((256, 256), lambda i, p: (0, (p[0] * 2 + p[1]) * 8 + i))]
            + [pl.BlockSpec((v.shape[0], 256), lambda i, p: (0, i)) for v in pieces]
            + [pl.BlockSpec(v.shape, whole) for v in grads],
            out_specs=pl.BlockSpec((256, 512), lambda i, p: (i, 0)),
        ),
        out_shape=jax.ShapeDtypeStruct((2048, 512), BF),
        compiler_params=params(16),
        cost_estimate=cost(2 * 1024 * 2048 * 512, 8 << 20),
        name="weight_grad",
    )(place, tokens, *pieces, *grads)


def sum_spread_kernel(scale, parts, out):
    total = parts[0].astype(F32)
    for k in range(1, parts.shape[0]):
        total = total + parts[k].astype(F32)
    low = (total * scale).astype(BF)
    for k in range(parts.shape[0]):
        out[k] = low


def sum_spread(parts, scale):
    count, rows, width = parts.shape
    block = pl.BlockSpec((count, rows // 4, width), lambda i: (0, i, 0))
    return pl.pallas_call(
        functools.partial(sum_spread_kernel, scale),
        grid=(4,),
        in_specs=[block],
        out_specs=block,
        out_shape=jax.ShapeDtypeStruct(parts.shape, BF),
        compiler_params=params(8),
        cost_estimate=cost(2 << 20, 4 << 20),
        name="sum_spread",
    )(parts)


def join_kernel(place, mine, other, out):
    first = pl.program_id(0) < 2
    own = first == (place[1] == 0)

    @pl.when(own)
    def _():
        out[...] = mine[...]

    @pl.when(jnp.logical_not(own))
    def _():
        out[...] = other[...]


def join_cores(place, mine, other):
    rows, width = mine.shape
    step = rows // 2

    def mine_block(i, p):
        return (jnp.where((i < 2) == (p[1] == 0), i % 2, jnp.where(i < 2, 0, 1)), 0)

    def other_block(i, p):
        return (jnp.where((i < 2) == (p[1] == 0), jnp.where(i < 2, 0, 1), i % 2), 0)

    return pl.pallas_call(
        join_kernel,
        grid_spec=pltpu.PrefetchScalarGridSpec(
            num_scalar_prefetch=1,
            grid=(4,),
            in_specs=[pl.BlockSpec((step, width), mine_block), pl.BlockSpec((step, width), other_block)],
            out_specs=pl.BlockSpec((step, width), lambda i, p: (i, 0)),
        ),
        out_shape=jax.ShapeDtypeStruct((2 * rows, width), BF),
        compiler_params=params(10),
        cost_estimate=cost(1 << 20, 8 << 20),
        name="join_cores",
    )(place, mine, other)


def swap_core(xh, y, core, xl, z):
    return xh, y, 1 - core, xl, z


def next_rows(step):
    def where(xh, y, core, xl, z):
        seq = xh * 8 + y * 2 + core + step
        if seq < 0 or seq > 15:
            return None
        return seq // 8, (seq // 2) % 4, seq % 2, xl, z

    return where


def shards(queries, hidden, key_weight, doc_lengths, entropy_cot):
    tokens = hidden[0]
    rows, model = tokens.shape
    half, width = key_weight.shape
    fsdp, core = lax.axis_index("xl"), lax.axis_index("core")
    seq = lax.axis_index(("xh", "y", "core"))
    place = jnp.stack([fsdp, core, seq]).astype(jnp.int32)

    mine = lax.dynamic_slice_in_dim(key_weight, core * (half // 2), half // 2, 0)
    fetch = lambda xh, y, core, xl, z: along_x(xh, y, core, xl, z, 1 - 2 * core)
    got = [move(mine[k * half // 4:(k + 1) * half // 4], fetch) for k in range(2)]
    total = project_own(place, tokens, key_weight)

    quarter = model // 4

    def column(first, last, is_fsdp, is_core):
        start = (is_fsdp * 2 + is_core) * quarter
        return lax.dynamic_slice(tokens, (first, start), (last - first, quarter))

    split = rows // 2
    routes = [swap_core]
    for step in (1, -1):
        for other in (0, 1):
            routes.append(functools.partial(along_x, step=step, other=other))
    columns = [column(0, rows, fsdp, 1 - core)]
    for k, route in enumerate(routes[1:]):
        first = 0 if k < 2 else split
        columns.append(column(first, first + split, 1 - fsdp, core if k % 2 == 0 else 1 - core))

    got[0], total, columns = lax.optimization_barrier((got[0], total, columns))
    swapped = [move(v, swap_core) for v in got]
    total = project_add(place, tokens, got[:1], [(False, 0)], total, F32)
    total = project_add(place, tokens, got[1:], [(False, 1)], total, F32)
    key_own = project_add(place, tokens, swapped, [(True, 0), (True, 1)], total, BF)
    key_halo = move(key_own, next_rows(1))

    columns, _ = lax.optimization_barrier((columns, got[1]))
    pieces = [move(v, route) for v, route in zip(columns, routes)]

    entropy, grad_query, grad_own, grad_halo = attend(
        place, doc_lengths, queries[0], key_own, key_halo, entropy_cot[0].T
    )

    grad_halo, pieces = lax.optimization_barrier((grad_halo, pieces))
    from_next = move(grad_halo, next_rows(-1))
    key_grad = (grad_own + from_next.astype(F32)).astype(BF)
    grads = [key_grad, move(key_grad, routes[0])]
    for k, route in enumerate(routes[1:]):
        first = 0 if k < 2 else split
        grads.append(move(key_grad[first:first + split], route))

    chips = ("xh", "y", "z")
    parts = weight_grad(place, tokens, pieces, grads).reshape(32, 64, width)
    parts = lax.all_to_all(parts, chips, split_axis=0, concat_axis=0, tiled=True)
    spread = sum_spread(parts, (rows * 16 * 8) ** (-0.5))
    final = lax.all_to_all(spread, chips, split_axis=0, concat_axis=0, tiled=True).reshape(2048, width)
    other = move(final, swap_core)
    grad_weight = join_cores(place, final, other)
    return entropy.T[None], grad_query[None], grad_weight


def solution(mesh):
    fine = Mesh(mesh.devices.reshape(2, 4, 2, 2, 4), AXES)
    seq = ("xh", "y", "core")
    both = ("xl", "z")
    return jax.shard_map(
        shards,
        mesh=fine,
        in_specs=(
            P(both, seq, None),
            P(both, seq, None),
            P("xl", None),
            P(both, None),
            P(both, seq, None),
        ),
        out_specs=(P(both, seq, None), P(both, seq, None), P("xl", None)),
        check_vma=False,
    )
```

```python
import functools
import math

import jax
import jax.numpy as jnp
from jax import lax
from jax.experimental import pallas as pl
from jax.experimental.pallas import tpu as pltpu
from jax.sharding import Mesh, PartitionSpec as P

QH = 32
KVH = 4
HD = 128
GROUP = QH // KVH
BF = jnp.bfloat16
F32 = jnp.float32
AXES = ("xh", "y", "core", "xl", "z")
FACTOR = HD ** (-0.5)
EXP_SCALE = FACTOR * math.log2(math.e)
NEG = -1e30


def coords(index):
    seq, rest = divmod(index, 8)
    fsdp, z = divmod(rest, 4)
    return seq // 8, (seq // 2) % 4, seq % 2, fsdp, z


def linear(xh, y, core, xl, z):
    return ((xh * 8 + y * 2 + core) * 2 + xl) * 4 + z


def move(value, where):
    pairs = []
    for index in range(128):
        target = where(*coords(index))
        if target is not None:
            pairs.append((index, linear(*target)))
    return lax.ppermute(value, AXES, pairs)


def along_x(xh, y, core, xl, z, step, other=0):
    x = (xh * 2 + xl + step) % 4
    return x // 2, y, core ^ other, x % 2, z


def params(mib):
    return pltpu.CompilerParams(vmem_limit_bytes=mib << 20)


def cost(flops, moved):
    return pl.CostEstimate(flops=int(flops), bytes_accessed=int(moved), transcendentals=0)


def own_half_kernel(place, hidden, weight, out):
    @pl.when(pl.program_id(0) == 0)
    def _():
        out[...] = jnp.zeros_like(out)

    out[...] += jnp.dot(hidden[...], weight[...], preferred_element_type=F32)


def project_own(place, tokens, weight):
    rows, model = tokens.shape
    half, width = weight.shape
    step = half // 4
    return pl.pallas_call(
        own_half_kernel,
        grid_spec=pltpu.PrefetchScalarGridSpec(
            num_scalar_prefetch=1,
            grid=(4,),
            in_specs=[
                pl.BlockSpec((rows, step), lambda i, p: (0, p[0] * 4 + i)),
                pl.BlockSpec((step, width), lambda i, p: (i, 0)),
            ],
            out_specs=pl.BlockSpec((rows, width), lambda i, p: (0, 0)),
        ),
        out_shape=jax.ShapeDtypeStruct((rows, width), F32),
        compiler_params=params(8),
        cost_estimate=cost(2 * rows * half * width, 6 << 20),
        name="project_own",
    )(place, tokens, weight)


def near_kernel(low, high, weight, low_out, high_out, total):
    rows = jnp.concatenate([low[...], high[...]], axis=0)
    part = jnp.dot(rows, weight[...], preferred_element_type=F32)

    @pl.when(pl.program_id(0) == 0)
    def _():
        total[...] = part

    @pl.when(pl.program_id(0) > 0)
    def _():
        total[...] += part

    @pl.when(pl.program_id(0) == pl.num_programs(0) - 1)
    def _():
        count = low.shape[0]
        low_out[...] = total[:count]
        high_out[...] = total[count:]


def project_near(low, high, weight):
    rows = low.shape[0]
    half, width = weight.shape
    step = half // 4
    return pl.pallas_call(
        near_kernel,
        grid=(4,),
        in_specs=[
            pl.BlockSpec((rows, step), lambda i: (0, i)),
            pl.BlockSpec((rows, step), lambda i: (0, i)),
            pl.BlockSpec((step, width), lambda i: (i, 0)),
        ],
        out_specs=[pl.BlockSpec((rows, width), lambda i: (0, 0))] * 2,
        out_shape=[jax.ShapeDtypeStruct((rows, width), F32)] * 2,
        scratch_shapes=[pltpu.VMEM((2 * rows, width), F32)],
        compiler_params=params(12),
        cost_estimate=cost(4 * rows * half * width, 6 << 20),
        name="project_near",
    )(low, high, weight)


def attend_kernel(place, lengths, query, key_own, key_halo, weight, entropy, grad_query, grad_own,
                  grad_halo, bias, keys, keys_t):
    @pl.when(pl.program_id(0) == 0)
    def _():
        base = place[2] * 256
        position = base + lax.broadcasted_iota(jnp.int32, (8, 256), 1)

        def add(i, state):
            end, first = state
            end = end + lengths[0, i]
            return end, jnp.where(position >= end, end, first)

        _, first = lax.fori_loop(
            0, lengths.shape[1], add, (jnp.int32(0), jnp.zeros((8, 256), jnp.int32))
        )
        for half in range(2):
            begin = first[0:1, half * 128:(half + 1) * 128]
            here = position[0:1, half * 128:(half + 1) * 128]
            there = base - 256 + half * 128 + lax.broadcasted_iota(jnp.int32, (384, 128), 0)
            seen = (there >= begin) & (there <= here)
            value = jnp.where(seen, 0.0, NEG)
            bias[half, :, 0:128] = value
            bias[half, :, 128:256] = value

    keys[0:256, :] = key_halo[...]
    keys[256:512, :] = key_own[...]
    keys_t[...] = keys[...].T
    weights = weight[...].astype(F32)
    sums = [None, None]
    for pair in range(GROUP // 2):
        cols = [slice((2 * pair + k) * HD, (2 * pair + k + 1) * HD) for k in range(2)]
        for half in range(2):
            rows = slice(half * 128, (half + 1) * 128)
            window = slice(half * 128, half * 128 + 384)
            stack = jnp.concatenate([query[rows, cols[0]], query[rows, cols[1]]], axis=0)
            raw = lax.dot_general(
                keys[window, :], stack, (((1,), (1,)), ((), ())), preferred_element_type=F32
            ) + bias[half]
            top = jnp.max(raw, axis=0, keepdims=True)
            gap = raw - top
            power = jnp.exp2(gap * EXP_SCALE)
            den = jnp.sum(power, axis=0, keepdims=True)
            mean = jnp.sum(power * gap, axis=0, keepdims=True) / den
            row_weight = jnp.concatenate(
                [weights[2 * pair:2 * pair + 1, rows], weights[2 * pair + 1:2 * pair + 2, rows]], axis=1
            )
            slope_b = row_weight * FACTOR / den
            slope_a = slope_b * mean
            slope = (power * (slope_a - slope_b * gap)).astype(BF)
            level = jnp.log(den) - FACTOR * mean
            entropy[2 * pair:2 * pair + 1, rows] = level[:, 0:128]
            entropy[2 * pair + 1:2 * pair + 2, rows] = level[:, 128:256]
            turned = jnp.dot(keys_t[:, window], slope, preferred_element_type=F32) * FACTOR
            straight = turned.T.astype(BF)
            grad_query[rows, cols[0]] = straight[0:128]
            grad_query[rows, cols[1]] = straight[128:256]
            part = jnp.dot(slope, stack, preferred_element_type=F32)
            sums[half] = part if sums[half] is None else sums[half] + part
    low, high = sums
    grad_halo[0:128, :] = (low[0:128] * FACTOR).astype(grad_halo.dtype)
    grad_halo[128:256, :] = ((low[128:256] + high[0:128]) * FACTOR).astype(grad_halo.dtype)
    grad_own[0:128, :] = (low[256:384] + high[128:256]) * FACTOR
    grad_own[128:256, :] = high[256:384] * FACTOR


def attend(place, lengths, queries, key_own, key_halo, weight):
    rows, width = queries.shape
    wide = GROUP * HD
    by_head = lambda j, p, l: (0, j)
    return pl.pallas_call(
        attend_kernel,
        grid_spec=pltpu.PrefetchScalarGridSpec(
            num_scalar_prefetch=2,
            grid=(KVH,),
            in_specs=[
                pl.BlockSpec((rows, wide), by_head),
                pl.BlockSpec((rows, HD), by_head),
                pl.BlockSpec((rows, HD), by_head),
                pl.BlockSpec((GROUP, rows), lambda j, p, l: (j, 0)),
            ],
            out_specs=[
                pl.BlockSpec((GROUP, rows), lambda j, p, l: (j, 0)),
                pl.BlockSpec((rows, wide), by_head),
                pl.BlockSpec((rows, HD), by_head),
                pl.BlockSpec((rows, HD), by_head),
            ],
            scratch_shapes=[
                pltpu.VMEM((2, 384, 256), F32),
                pltpu.VMEM((512, HD), BF),
                pltpu.VMEM((HD, 512), BF),
            ],
        ),
        out_shape=[
            jax.ShapeDtypeStruct((QH, rows), F32),
            jax.ShapeDtypeStruct((rows, width), BF),
            jax.ShapeDtypeStruct((rows, KVH * HD), F32),
            jax.ShapeDtypeStruct((rows, KVH * HD), BF),
        ],
        compiler_params=params(16),
        cost_estimate=cost(4 << 30, 6 << 20),
        name="attend",
    )(place, lengths, queries, key_own, key_halo, weight)


def weight_grad_kernel(count, place, *refs):
    hidden, grads, out = refs[:count], refs[count:-1], refs[-1]
    rows = jnp.concatenate([piece[...] for piece in hidden], axis=0)
    grad = jnp.concatenate([piece[...] for piece in grads], axis=0)
    total = lax.dot_general(rows, grad, (((0,), (0,)), ((), ())), preferred_element_type=F32)
    out[...] = total.astype(BF)


def weight_grad(place, tokens, near, swapped, grads):
    whole = lambda i, p: (0, 0)
    return pl.pallas_call(
        functools.partial(weight_grad_kernel, 1 + len(near) + len(swapped)),
        grid_spec=pltpu.PrefetchScalarGridSpec(
            num_scalar_prefetch=1,
            grid=(8,),
            in_specs=[pl.BlockSpec((256, 256), lambda i, p: (0, (p[0] * 2 + p[1]) * 8 + i))]
            + [pl.BlockSpec((v.shape[0], 256), lambda i, p: (0, p[1] * 8 + i)) for v in near]
            + [pl.BlockSpec((v.shape[0], 256), lambda i, p: (0, i)) for v in swapped]
            + [pl.BlockSpec(v.shape, whole) for v in grads],
            out_specs=pl.BlockSpec((256, 512), lambda i, p: (i, 0)),
        ),
        out_shape=jax.ShapeDtypeStruct((2048, 512), BF),
        compiler_params=params(16),
        cost_estimate=cost(2 * 1024 * 2048 * 512, 8 << 20),
        name="weight_grad",
    )(place, tokens, *near, *swapped, *grads)


def sum_spread_kernel(scale, parts, out):
    total = parts[0].astype(F32)
    for k in range(1, parts.shape[0]):
        total = total + parts[k].astype(F32)
    low = (total * scale).astype(BF)
    for k in range(parts.shape[0]):
        out[k] = low


def sum_spread(parts, scale):
    count, rows, width = parts.shape
    block = pl.BlockSpec((count, rows // 4, width), lambda i: (0, i, 0))
    return pl.pallas_call(
        functools.partial(sum_spread_kernel, scale),
        grid=(4,),
        in_specs=[block],
        out_specs=block,
        out_shape=jax.ShapeDtypeStruct(parts.shape, BF),
        compiler_params=params(8),
        cost_estimate=cost(2 << 20, 4 << 20),
        name="sum_spread",
    )(parts)


def copy_kernel(place, rows, *refs):
    refs[-1][...] = rows[...]


def write_rows(place, rows, side, held=None):
    count, width = rows.shape
    step = count // 2
    more = {} if held is None else {"input_output_aliases": {2: 0}}
    return pl.pallas_call(
        copy_kernel,
        grid_spec=pltpu.PrefetchScalarGridSpec(
            num_scalar_prefetch=1,
            grid=(2,),
            in_specs=[pl.BlockSpec((step, width), lambda i, p: (i, 0))]
            + ([] if held is None else [pl.BlockSpec(memory_space=pl.ANY)]),
            out_specs=pl.BlockSpec(
                (step, width), lambda i, p: ((1 - p[1] if side else p[1]) * 2 + i, 0)
            ),
        ),
        out_shape=jax.ShapeDtypeStruct((2 * count, width), BF),
        compiler_params=params(8),
        cost_estimate=cost(1 << 20, 4 << 20),
        name="write_rows",
        **more,
    )(place, rows, *([] if held is None else [held]))


def swap_core(xh, y, core, xl, z):
    return xh, y, 1 - core, xl, z


def next_rows(step):
    def where(xh, y, core, xl, z):
        seq = xh * 8 + y * 2 + core + step
        if seq < 0 or seq > 15:
            return None
        return seq // 8, (seq // 2) % 4, seq % 2, xl, z

    return where


def shards(queries, hidden, key_weight, doc_lengths, entropy_cot):
    tokens = hidden[0]
    rows, model = tokens.shape
    half, width = key_weight.shape
    fsdp, core = lax.axis_index("xl"), lax.axis_index("core")
    seq = lax.axis_index(("xh", "y", "core"))
    place = jnp.stack([fsdp, core, seq]).astype(jnp.int32)

    quarter = model // 4
    split = rows // 2
    forward, backward = (functools.partial(along_x, step=step) for step in (1, -1))

    def column(first, last, start, count):
        return lax.dynamic_slice(tokens, (first, start), (last - first, count))

    near = [
        move(column(0, split, (1 - fsdp) * half, half), forward),
        move(column(split, rows, (1 - fsdp) * half, half), backward),
    ]
    passed = [column(0, rows, fsdp * half + (1 - core) * quarter, quarter)]
    total = project_own(place, tokens, key_weight)
    near, total, passed = lax.optimization_barrier((near, total, passed))
    low, high = project_near(*near, key_weight)
    low, high = move(low, backward), move(high, forward)
    key_own = (total + jnp.concatenate([low, high], axis=0)).astype(BF)
    key_halo = move(key_own, next_rows(1))

    start = (1 - core) * quarter
    passed += [lax.dynamic_slice(v, (0, start), (split, quarter)) for v in near]
    across = [move(v, swap_core) for v in passed]

    entropy, grad_query, grad_own, grad_halo = attend(
        place, doc_lengths, queries[0], key_own, key_halo, entropy_cot[0].T
    )

    grad_halo, across = lax.optimization_barrier((grad_halo, across))
    from_next = move(grad_halo, next_rows(-1))
    key_grad = (grad_own + from_next.astype(F32)).astype(BF)
    grad_near = [move(key_grad[:split], forward), move(key_grad[split:], backward)]
    grads = [key_grad, *grad_near, move(key_grad, swap_core)]
    grads += [move(v, swap_core) for v in grad_near]

    chips = ("xh", "y", "z")
    parts = weight_grad(place, tokens, near, across, grads).reshape(32, 64, width)
    parts = lax.all_to_all(parts, chips, split_axis=0, concat_axis=0, tiled=True)
    spread = sum_spread(parts, (rows * 16 * 8) ** (-0.5))
    final = lax.all_to_all(spread, chips, split_axis=0, concat_axis=0, tiled=True).reshape(2048, width)
    other = move(final, swap_core)
    grad_weight = write_rows(place, other, 1, write_rows(place, final, 0))
    return entropy.T[None], grad_query[None], grad_weight


def solution(mesh):
    fine = Mesh(mesh.devices.reshape(2, 4, 2, 2, 4), AXES)
    seq = ("xh", "y", "core")
    both = ("xl", "z")
    return jax.shard_map(
        shards,
        mesh=fine,
        in_specs=(
            P(both, seq, None),
            P(both, seq, None),
            P("xl", None),
            P(both, None),
            P(both, seq, None),
        ),
        out_specs=(P(both, seq, None), P(both, seq, None), P("xl", None)),
        check_vma=False,
    )
```

```python
import functools
import math

import jax
import jax.numpy as jnp
from jax import lax
from jax.experimental import pallas as pl
from jax.experimental.pallas import tpu as pltpu
from jax.sharding import Mesh, PartitionSpec as P

QH = 32
KVH = 4
HD = 128
GROUP = QH // KVH
BF = jnp.bfloat16
F32 = jnp.float32
AXES = ("xh", "y", "core", "xl", "z")
FACTOR = HD ** (-0.5)
EXP_SCALE = FACTOR * math.log2(math.e)
NEG = -1e30


def coords(index):
    seq, rest = divmod(index, 8)
    fsdp, z = divmod(rest, 4)
    return seq // 8, (seq // 2) % 4, seq % 2, fsdp, z


def linear(xh, y, core, xl, z):
    return ((xh * 8 + y * 2 + core) * 2 + xl) * 4 + z


def move(value, where):
    pairs = []
    for index in range(128):
        target = where(*coords(index))
        if target is not None:
            pairs.append((index, linear(*target)))
    return lax.ppermute(value, AXES, pairs)


def along_x(xh, y, core, xl, z, step, other=0):
    x = (xh * 2 + xl + step) % 4
    return x // 2, y, core ^ other, x % 2, z


def params(mib):
    return pltpu.CompilerParams(vmem_limit_bytes=mib << 20)


def cost(flops, moved):
    return pl.CostEstimate(flops=int(flops), bytes_accessed=int(moved), transcendentals=0)


def own_half_kernel(place, hidden, weight, out):
    @pl.when(pl.program_id(0) == 0)
    def _():
        out[...] = jnp.zeros_like(out)

    out[...] += jnp.dot(hidden[...], weight[...], preferred_element_type=F32)


def project_own(place, tokens, weight):
    rows, model = tokens.shape
    half, width = weight.shape
    step = half // 4
    return pl.pallas_call(
        own_half_kernel,
        grid_spec=pltpu.PrefetchScalarGridSpec(
            num_scalar_prefetch=1,
            grid=(4,),
            in_specs=[
                pl.BlockSpec((rows, step), lambda i, p: (0, p[0] * 4 + i)),
                pl.BlockSpec((step, width), lambda i, p: (i, 0)),
            ],
            out_specs=pl.BlockSpec((rows, width), lambda i, p: (0, 0)),
        ),
        out_shape=jax.ShapeDtypeStruct((rows, width), F32),
        compiler_params=params(8),
        cost_estimate=cost(2 * rows * half * width, 6 << 20),
        name="project_own",
    )(place, tokens, weight)


def near_kernel(low, high, weight, low_out, high_out, total):
    rows = jnp.concatenate([low[...], high[...]], axis=0)
    part = jnp.dot(rows, weight[...], preferred_element_type=F32)

    @pl.when(pl.program_id(0) == 0)
    def _():
        total[...] = part

    @pl.when(pl.program_id(0) > 0)
    def _():
        total[...] += part

    @pl.when(pl.program_id(0) == pl.num_programs(0) - 1)
    def _():
        count = low.shape[0]
        low_out[...] = total[:count].astype(BF)
        high_out[...] = total[count:].astype(BF)


def project_near(low, high, weight):
    rows = low.shape[0]
    half, width = weight.shape
    step = half // 4
    return pl.pallas_call(
        near_kernel,
        grid=(4,),
        in_specs=[
            pl.BlockSpec((rows, step), lambda i: (0, i)),
            pl.BlockSpec((rows, step), lambda i: (0, i)),
            pl.BlockSpec((step, width), lambda i: (i, 0)),
        ],
        out_specs=[pl.BlockSpec((rows, width), lambda i: (0, 0))] * 2,
        out_shape=[jax.ShapeDtypeStruct((rows, width), BF)] * 2,
        scratch_shapes=[pltpu.VMEM((2 * rows, width), F32)],
        compiler_params=params(12),
        cost_estimate=cost(4 * rows * half * width, 6 << 20),
        name="project_near",
    )(low, high, weight)


def attend_kernel(place, lengths, query, key_own, key_halo, weight, entropy, grad_query, grad_own,
                  grad_halo, bias, keys, keys_t):
    @pl.when(pl.program_id(0) == 0)
    def _():
        base = place[2] * 256
        position = base + lax.broadcasted_iota(jnp.int32, (8, 256), 1)

        def add(i, state):
            end, first = state
            end = end + lengths[0, i]
            return end, jnp.where(position >= end, end, first)

        _, first = lax.fori_loop(
            0, lengths.shape[1], add, (jnp.int32(0), jnp.zeros((8, 256), jnp.int32))
        )
        for half in range(2):
            begin = first[0:1, half * 128:(half + 1) * 128]
            here = position[0:1, half * 128:(half + 1) * 128]
            there = base - 256 + half * 128 + lax.broadcasted_iota(jnp.int32, (384, 128), 0)
            seen = (there >= begin) & (there <= here)
            value = jnp.where(seen, 0.0, NEG)
            bias[half, :, 0:128] = value
            bias[half, :, 128:256] = value

    keys[0:256, :] = key_halo[...]
    keys[256:512, :] = key_own[...]
    keys_t[...] = keys[...].T
    weights = weight[...].astype(F32)
    def score(pair, half):
        cols = [slice((2 * pair + k) * HD, (2 * pair + k + 1) * HD) for k in range(2)]
        rows = slice(half * 128, (half + 1) * 128)
        window = slice(half * 128, half * 128 + 384)
        stack = jnp.concatenate([query[rows, cols[0]], query[rows, cols[1]]], axis=0)
        raw = lax.dot_general(
            keys[window, :], stack, (((1,), (1,)), ((), ())), preferred_element_type=F32
        ) + bias[half]
        return raw, stack

    def soften(pair, half, raw):
        rows = slice(half * 128, (half + 1) * 128)
        top = jnp.max(raw, axis=0, keepdims=True)
        gap = raw - top
        power = jnp.exp2(gap * EXP_SCALE)
        den = jnp.sum(power, axis=0, keepdims=True)
        mean = jnp.sum(power * gap, axis=0, keepdims=True) / den
        row_weight = jnp.concatenate(
            [weights[2 * pair:2 * pair + 1, rows], weights[2 * pair + 1:2 * pair + 2, rows]], axis=1
        )
        slope_b = row_weight * FACTOR / den
        slope_a = slope_b * mean
        level = jnp.log(den) - FACTOR * mean
        entropy[2 * pair:2 * pair + 1, rows] = level[:, 0:128]
        entropy[2 * pair + 1:2 * pair + 2, rows] = level[:, 128:256]
        return (power * (slope_a - slope_b * gap)).astype(BF)

    def grads(pair, half, slope, stack):
        cols = [slice((2 * pair + k) * HD, (2 * pair + k + 1) * HD) for k in range(2)]
        rows = slice(half * 128, (half + 1) * 128)
        window = slice(half * 128, half * 128 + 384)
        turned = jnp.dot(keys_t[:, window], slope, preferred_element_type=F32) * FACTOR
        straight = turned.T.astype(BF)
        grad_query[rows, cols[0]] = straight[0:128]
        grad_query[rows, cols[1]] = straight[128:256]
        part = jnp.dot(slope, stack, preferred_element_type=F32)
        sums[half] = part if sums[half] is None else sums[half] + part

    sums = [None, None]
    order = [(pair, half) for pair in range(GROUP // 2) for half in range(2)]
    ahead = score(*order[0])
    last = None
    for i, at in enumerate(order):
        raw, stack = ahead
        if i + 1 < len(order):
            ahead = score(*order[i + 1])
        if last is not None:
            grads(*last)
        last = (*at, soften(*at, raw), stack)
    grads(*last)
    low, high = sums
    grad_halo[0:128, :] = (low[0:128] * FACTOR).astype(grad_halo.dtype)
    grad_halo[128:256, :] = ((low[128:256] + high[0:128]) * FACTOR).astype(grad_halo.dtype)
    grad_own[0:128, :] = (low[256:384] + high[128:256]) * FACTOR
    grad_own[128:256, :] = high[256:384] * FACTOR


def attend(place, lengths, queries, key_own, key_halo, weight):
    rows, width = queries.shape
    wide = GROUP * HD
    by_head = lambda j, p, l: (0, j)
    return pl.pallas_call(
        attend_kernel,
        grid_spec=pltpu.PrefetchScalarGridSpec(
            num_scalar_prefetch=2,
            grid=(KVH,),
            in_specs=[
                pl.BlockSpec((rows, wide), by_head),
                pl.BlockSpec((rows, HD), by_head),
                pl.BlockSpec((rows, HD), by_head),
                pl.BlockSpec((GROUP, rows), lambda j, p, l: (j, 0)),
            ],
            out_specs=[
                pl.BlockSpec((GROUP, rows), lambda j, p, l: (j, 0)),
                pl.BlockSpec((rows, wide), by_head),
                pl.BlockSpec((rows, HD), by_head),
                pl.BlockSpec((rows, HD), by_head),
            ],
            scratch_shapes=[
                pltpu.VMEM((2, 384, 256), F32),
                pltpu.VMEM((512, HD), BF),
                pltpu.VMEM((HD, 512), BF),
            ],
        ),
        out_shape=[
            jax.ShapeDtypeStruct((QH, rows), F32),
            jax.ShapeDtypeStruct((rows, width), BF),
            jax.ShapeDtypeStruct((rows, KVH * HD), F32),
            jax.ShapeDtypeStruct((rows, KVH * HD), BF),
        ],
        compiler_params=params(16),
        cost_estimate=cost(4 << 30, 6 << 20),
        name="attend",
    )(place, lengths, queries, key_own, key_halo, weight)


def weight_grad_kernel(count, place, *refs):
    hidden, grads, out = refs[:count], refs[count:-1], refs[-1]
    rows = jnp.concatenate([piece[...] for piece in hidden], axis=0)
    grad = jnp.concatenate([piece[...] for piece in grads], axis=0)
    total = lax.dot_general(rows, grad, (((0,), (0,)), ((), ())), preferred_element_type=F32)
    out[...] = total.astype(BF)


def weight_grad(place, tokens, near, swapped, grads):
    whole = lambda i, p: (0, 0)
    return pl.pallas_call(
        functools.partial(weight_grad_kernel, 1 + len(near) + len(swapped)),
        grid_spec=pltpu.PrefetchScalarGridSpec(
            num_scalar_prefetch=1,
            grid=(4,),
            in_specs=[pl.BlockSpec((256, 512), lambda i, p: (0, (p[0] * 2 + p[1]) * 4 + i))]
            + [pl.BlockSpec((v.shape[0], 512), lambda i, p: (0, p[1] * 4 + i)) for v in near]
            + [pl.BlockSpec((v.shape[0], 512), lambda i, p: (0, i)) for v in swapped]
            + [pl.BlockSpec(v.shape, whole) for v in grads],
            out_specs=pl.BlockSpec((512, 512), lambda i, p: (i, 0)),
        ),
        out_shape=jax.ShapeDtypeStruct((2048, 512), BF),
        compiler_params=params(16),
        cost_estimate=cost(2 * 1024 * 2048 * 512, 8 << 20),
        name="weight_grad",
    )(place, tokens, *near, *swapped, *grads)


def sum_spread_kernel(scale, parts, out):
    total = parts[0].astype(F32)
    for k in range(1, parts.shape[0]):
        total = total + parts[k].astype(F32)
    low = (total * scale).astype(BF)
    for k in range(parts.shape[0]):
        out[k] = low


def sum_spread(parts, scale):
    count, rows, width = parts.shape
    block = pl.BlockSpec((count, rows // 4, width), lambda i: (0, i, 0))
    return pl.pallas_call(
        functools.partial(sum_spread_kernel, scale),
        grid=(4,),
        in_specs=[block],
        out_specs=block,
        out_shape=jax.ShapeDtypeStruct(parts.shape, BF),
        compiler_params=params(8),
        cost_estimate=cost(2 << 20, 4 << 20),
        name="sum_spread",
    )(parts)


def copy_kernel(place, rows, *refs):
    refs[-1][...] = rows[...]


def write_rows(place, rows, side, held=None):
    count, width = rows.shape
    step = count // 2
    more = {} if held is None else {"input_output_aliases": {2: 0}}
    return pl.pallas_call(
        copy_kernel,
        grid_spec=pltpu.PrefetchScalarGridSpec(
            num_scalar_prefetch=1,
            grid=(2,),
            in_specs=[pl.BlockSpec((step, width), lambda i, p: (i, 0))]
            + ([] if held is None else [pl.BlockSpec(memory_space=pl.ANY)]),
            out_specs=pl.BlockSpec(
                (step, width), lambda i, p: ((1 - p[1] if side else p[1]) * 2 + i, 0)
            ),
        ),
        out_shape=jax.ShapeDtypeStruct((2 * count, width), BF),
        compiler_params=params(8),
        cost_estimate=cost(1 << 20, 4 << 20),
        name="write_rows",
        **more,
    )(place, rows, *([] if held is None else [held]))


def swap_core(xh, y, core, xl, z):
    return xh, y, 1 - core, xl, z


def next_rows(step):
    def where(xh, y, core, xl, z):
        seq = xh * 8 + y * 2 + core + step
        if seq < 0 or seq > 15:
            return None
        return seq // 8, (seq // 2) % 4, seq % 2, xl, z

    return where


def shards(queries, hidden, key_weight, doc_lengths, entropy_cot):
    tokens = hidden[0]
    rows, model = tokens.shape
    half, width = key_weight.shape
    fsdp, core = lax.axis_index("xl"), lax.axis_index("core")
    seq = lax.axis_index(("xh", "y", "core"))
    place = jnp.stack([fsdp, core, seq]).astype(jnp.int32)

    quarter = model // 4
    split = rows // 2
    forward, backward = (functools.partial(along_x, step=step) for step in (1, -1))

    def column(first, last, start, count):
        return lax.dynamic_slice(tokens, (first, start), (last - first, count))

    near = [
        move(column(0, split, (1 - fsdp) * half, half), forward),
        move(column(split, rows, (1 - fsdp) * half, half), backward),
    ]
    passed = [column(0, rows, fsdp * half + (1 - core) * quarter, quarter)]
    total = project_own(place, tokens, key_weight)
    near, total, passed = lax.optimization_barrier((near, total, passed))
    low, high = project_near(*near, key_weight)
    low, high = move(low, backward), move(high, forward)
    key_own = (total + jnp.concatenate([low, high], axis=0).astype(F32)).astype(BF)
    key_halo = move(key_own, next_rows(1))

    start = (1 - core) * quarter
    passed += [lax.dynamic_slice(v, (0, start), (split, quarter)) for v in near]
    across = [move(v, swap_core) for v in passed]

    entropy, grad_query, grad_own, grad_halo = attend(
        place, doc_lengths, queries[0], key_own, key_halo, entropy_cot[0].T
    )

    grad_halo, across = lax.optimization_barrier((grad_halo, across))
    from_next = move(grad_halo, next_rows(-1))
    key_grad = (grad_own + from_next.astype(F32)).astype(BF)
    grad_near = [move(key_grad[:split], forward), move(key_grad[split:], backward)]
    grads = [key_grad, *grad_near, move(key_grad, swap_core)]
    grads += [move(v, swap_core) for v in grad_near]

    chips = ("xh", "y", "z")
    parts = weight_grad(place, tokens, near, across, grads).reshape(32, 64, width)
    parts = lax.all_to_all(parts, chips, split_axis=0, concat_axis=0, tiled=True)
    spread = sum_spread(parts, (rows * 16 * 8) ** (-0.5))
    final = lax.all_to_all(spread, chips, split_axis=0, concat_axis=0, tiled=True).reshape(2048, width)
    other = move(final, swap_core)
    grad_weight = write_rows(place, other, 1, write_rows(place, final, 0))
    return entropy.T[None], grad_query[None], grad_weight


def solution(mesh):
    fine = Mesh(mesh.devices.reshape(2, 4, 2, 2, 4), AXES)
    seq = ("xh", "y", "core")
    both = ("xl", "z")
    return jax.shard_map(
        shards,
        mesh=fine,
        in_specs=(
            P(both, seq, None),
            P(both, seq, None),
            P("xl", None),
            P(both, None),
            P(both, seq, None),
        ),
        out_specs=(P(both, seq, None), P(both, seq, None), P("xl", None)),
        check_vma=False,
    )
```

```python
import functools
import math

import jax
import jax.numpy as jnp
from jax import lax
from jax.experimental import pallas as pl
from jax.experimental.pallas import tpu as pltpu
from jax.sharding import Mesh, PartitionSpec as P

QH = 32
KVH = 4
HD = 128
GROUP = QH // KVH
BF = jnp.bfloat16
F32 = jnp.float32
AXES = ("xh", "y", "core", "xl", "z")
FACTOR = HD ** (-0.5)
EXP_SCALE = FACTOR * math.log2(math.e)
NEG = -1e30


def coords(index):
    seq, rest = divmod(index, 8)
    fsdp, z = divmod(rest, 4)
    return seq // 8, (seq // 2) % 4, seq % 2, fsdp, z


def linear(xh, y, core, xl, z):
    return ((xh * 8 + y * 2 + core) * 2 + xl) * 4 + z


def move(value, where):
    pairs = []
    for index in range(128):
        target = where(*coords(index))
        if target is not None:
            pairs.append((index, linear(*target)))
    return lax.ppermute(value, AXES, pairs)


def along_x(xh, y, core, xl, z, step, other=0):
    x = (xh * 2 + xl + step) % 4
    return x // 2, y, core ^ other, x % 2, z


def params(mib):
    return pltpu.CompilerParams(vmem_limit_bytes=mib << 20)


def cost(flops, moved):
    return pl.CostEstimate(flops=int(flops), bytes_accessed=int(moved), transcendentals=0)


def own_half_kernel(place, hidden, weight, out):
    @pl.when(pl.program_id(0) == 0)
    def _():
        out[...] = jnp.zeros_like(out)

    out[...] += jnp.dot(hidden[...], weight[...], preferred_element_type=F32)


def project_own(place, tokens, weight):
    rows, model = tokens.shape
    half, width = weight.shape
    step = half // 4
    return pl.pallas_call(
        own_half_kernel,
        grid_spec=pltpu.PrefetchScalarGridSpec(
            num_scalar_prefetch=1,
            grid=(4,),
            in_specs=[
                pl.BlockSpec((rows, step), lambda i, p: (0, p[0] * 4 + i)),
                pl.BlockSpec((step, width), lambda i, p: (i, 0)),
            ],
            out_specs=pl.BlockSpec((rows, width), lambda i, p: (0, 0)),
        ),
        out_shape=jax.ShapeDtypeStruct((rows, width), F32),
        compiler_params=params(8),
        cost_estimate=cost(2 * rows * half * width, 6 << 20),
        name="project_own",
    )(place, tokens, weight)


def near_kernel(low, high, weight, low_out, high_out, total):
    step = weight.shape[0] // 4
    count = low.shape[0]
    total[...] = jnp.zeros_like(total)

    @pl.loop(0, 4)
    def _(k):
        part = pl.ds(pl.multiple_of(k * step, step), step)
        rows = jnp.concatenate([low[:, part], high[:, part]], axis=0)
        total[...] += jnp.dot(rows, weight[part, :], preferred_element_type=F32)

    low_out[...] = total[:count].astype(BF)
    high_out[...] = total[count:].astype(BF)


def project_near(low, high, weight):
    rows = low.shape[0]
    half, width = weight.shape
    here = pl.BlockSpec(memory_space=pltpu.VMEM)
    return pl.pallas_call(
        near_kernel,
        in_specs=[here] * 3,
        out_specs=[here] * 2,
        out_shape=[jax.ShapeDtypeStruct((rows, width), BF)] * 2,
        scratch_shapes=[pltpu.VMEM((2 * rows, width), F32)],
        compiler_params=params(12),
        cost_estimate=cost(4 * rows * half * width, 6 << 20),
        name="project_near",
    )(low, high, weight)


def attend_kernel(place, lengths, query, key_own, key_halo, weight, entropy, grad_query, grad_own,
                  grad_halo, bias, keys, keys_t):
    @pl.when(pl.program_id(0) == 0)
    def _():
        base = place[2] * 256
        position = base + lax.broadcasted_iota(jnp.int32, (8, 256), 1)

        def add(i, state):
            end, first = state
            end = end + lengths[0, i]
            return end, jnp.where(position >= end, end, first)

        _, first = lax.fori_loop(
            0, lengths.shape[1], add, (jnp.int32(0), jnp.zeros((8, 256), jnp.int32))
        )
        for half in range(2):
            begin = first[0:1, half * 128:(half + 1) * 128]
            here = position[0:1, half * 128:(half + 1) * 128]
            there = base - 256 + half * 128 + lax.broadcasted_iota(jnp.int32, (384, 128), 0)
            seen = (there >= begin) & (there <= here)
            value = jnp.where(seen, 0.0, NEG)
            bias[half, :, 0:128] = value
            bias[half, :, 128:256] = value

    keys[0:256, :] = key_halo[...]
    keys[256:512, :] = key_own[...]
    keys_t[...] = keys[...].T
    weights = weight[...].astype(F32)
    def score(pair, half):
        cols = [slice((2 * pair + k) * HD, (2 * pair + k + 1) * HD) for k in range(2)]
        rows = slice(half * 128, (half + 1) * 128)
        window = slice(half * 128, half * 128 + 384)
        stack = jnp.concatenate([query[rows, cols[0]], query[rows, cols[1]]], axis=0)
        raw = lax.dot_general(
            keys[window, :], stack, (((1,), (1,)), ((), ())), preferred_element_type=F32
        ) + bias[half]
        return raw, stack

    def soften(pair, half, raw):
        rows = slice(half * 128, (half + 1) * 128)
        top = jnp.max(raw, axis=0, keepdims=True)
        gap = raw - top
        power = jnp.exp2(gap * EXP_SCALE)
        den = jnp.sum(power, axis=0, keepdims=True)
        mean = jnp.sum(power * gap, axis=0, keepdims=True) / den
        row_weight = jnp.concatenate(
            [weights[2 * pair:2 * pair + 1, rows], weights[2 * pair + 1:2 * pair + 2, rows]], axis=1
        )
        slope_b = row_weight * FACTOR / den
        slope_a = slope_b * mean
        level = jnp.log(den) - FACTOR * mean
        entropy[2 * pair:2 * pair + 1, rows] = level[:, 0:128]
        entropy[2 * pair + 1:2 * pair + 2, rows] = level[:, 128:256]
        return (power * (slope_a - slope_b * gap)).astype(BF)

    def grads(pair, half, slope, stack):
        cols = [slice((2 * pair + k) * HD, (2 * pair + k + 1) * HD) for k in range(2)]
        rows = slice(half * 128, (half + 1) * 128)
        window = slice(half * 128, half * 128 + 384)
        turned = jnp.dot(keys_t[:, window], slope, preferred_element_type=F32) * FACTOR
        straight = turned.T.astype(BF)
        grad_query[rows, cols[0]] = straight[0:128]
        grad_query[rows, cols[1]] = straight[128:256]
        part = jnp.dot(slope, stack, preferred_element_type=F32)
        sums[half] = part if sums[half] is None else sums[half] + part

    sums = [None, None]
    order = [(pair, half) for pair in range(GROUP // 2) for half in range(2)]
    ahead = score(*order[0])
    last = None
    for i, at in enumerate(order):
        raw, stack = ahead
        if i + 1 < len(order):
            ahead = score(*order[i + 1])
        if last is not None:
            grads(*last)
        last = (*at, soften(*at, raw), stack)
    grads(*last)
    low, high = sums
    grad_halo[0:128, :] = (low[0:128] * FACTOR).astype(grad_halo.dtype)
    grad_halo[128:256, :] = ((low[128:256] + high[0:128]) * FACTOR).astype(grad_halo.dtype)
    grad_own[0:128, :] = (low[256:384] + high[128:256]) * FACTOR
    grad_own[128:256, :] = high[256:384] * FACTOR


def attend(place, lengths, queries, key_own, key_halo, weight):
    rows, width = queries.shape
    wide = GROUP * HD
    by_head = lambda j, p, l: (0, j)
    return pl.pallas_call(
        attend_kernel,
        grid_spec=pltpu.PrefetchScalarGridSpec(
            num_scalar_prefetch=2,
            grid=(KVH,),
            in_specs=[
                pl.BlockSpec((rows, wide), by_head),
                pl.BlockSpec((rows, HD), by_head),
                pl.BlockSpec((rows, HD), by_head),
                pl.BlockSpec((GROUP, rows), lambda j, p, l: (j, 0)),
            ],
            out_specs=[
                pl.BlockSpec((GROUP, rows), lambda j, p, l: (j, 0)),
                pl.BlockSpec((rows, wide), by_head),
                pl.BlockSpec((rows, HD), by_head),
                pl.BlockSpec((rows, HD), by_head),
            ],
            scratch_shapes=[
                pltpu.VMEM((2, 384, 256), F32),
                pltpu.VMEM((512, HD), BF),
                pltpu.VMEM((HD, 512), BF),
            ],
        ),
        out_shape=[
            jax.ShapeDtypeStruct((QH, rows), F32),
            jax.ShapeDtypeStruct((rows, width), BF),
            jax.ShapeDtypeStruct((rows, KVH * HD), F32),
            jax.ShapeDtypeStruct((rows, KVH * HD), BF),
        ],
        compiler_params=params(16),
        cost_estimate=cost(4 << 30, 6 << 20),
        name="attend",
    )(place, lengths, queries, key_own, key_halo, weight)


def weight_grad_kernel(count, far, place, *refs):
    hidden, grads, out, grad = refs[:count], refs[count:-2], refs[-2], refs[-1]
    grad[...] = jnp.concatenate([piece[...] for piece in grads], axis=0)
    step = 512

    @pl.loop(0, out.shape[0] // step)
    def _(i):
        here = pl.multiple_of(i * step, step)
        there = pl.multiple_of(place[1] * out.shape[0] + i * step, step)
        rows = jnp.concatenate(
            [piece[:, pl.ds(there if far[k] else here, step)] for k, piece in enumerate(hidden)], axis=0
        )
        total = lax.dot_general(rows, grad[...], (((0,), (0,)), ((), ())), preferred_element_type=F32)
        out[pl.ds(here, step), :] = total.astype(BF)


def weight_grad(place, own, near, swapped, grads):
    here = pl.BlockSpec(memory_space=pltpu.VMEM)
    hidden = [own, *near, *swapped]
    far = [False] + [True] * len(near) + [False] * len(swapped)
    return pl.pallas_call(
        functools.partial(weight_grad_kernel, len(hidden), far),
        in_specs=[pl.BlockSpec(memory_space=pltpu.SMEM)] + [here] * (len(hidden) + len(grads)),
        out_specs=here,
        out_shape=jax.ShapeDtypeStruct((2048, 512), BF),
        scratch_shapes=[pltpu.VMEM((1024, 512), BF)],
        compiler_params=params(16),
        cost_estimate=cost(2 * 1024 * 2048 * 512, 8 << 20),
        name="weight_grad",
    )(place, *hidden, *grads)


def sum_spread_kernel(scale, parts, out):
    total = parts[0].astype(F32)
    for k in range(1, parts.shape[0]):
        total = total + parts[k].astype(F32)
    low = (total * scale).astype(BF)
    for k in range(parts.shape[0]):
        out[k] = low


def sum_spread(parts, scale):
    count, rows, width = parts.shape
    block = pl.BlockSpec((count, rows // 4, width), lambda i: (0, i, 0))
    return pl.pallas_call(
        functools.partial(sum_spread_kernel, scale),
        grid=(4,),
        in_specs=[block],
        out_specs=block,
        out_shape=jax.ShapeDtypeStruct(parts.shape, BF),
        compiler_params=params(8),
        cost_estimate=cost(2 << 20, 4 << 20),
        name="sum_spread",
    )(parts)


def copy_kernel(side, first, rows, *refs):
    out, done = refs[-2], refs[-1]
    core = lax.axis_index("core")
    start = (1 - core if side else core) * (out.shape[0] // 2) + first
    start = pl.multiple_of(start, rows.shape[0])
    copy = pltpu.make_async_copy(rows, out.at[pl.ds(start, rows.shape[0])], done)
    copy.start()
    copy.wait()


def write_rows(rows, total, side, first, held=None):
    count, width = rows.shape
    anywhere = pl.BlockSpec(memory_space=pl.ANY)
    given = [rows] if held is None else [rows, held]
    return pl.pallas_call(
        functools.partial(copy_kernel, side, first),
        in_specs=[anywhere] * len(given),
        out_specs=anywhere,
        out_shape=jax.ShapeDtypeStruct((total, width), BF),
        scratch_shapes=[pltpu.SemaphoreType.DMA],
        input_output_aliases={} if held is None else {1: 0},
        compiler_params=params(4),
        cost_estimate=cost(1 << 20, 4 << 20),
        name="write_rows",
    )(*given)


def swap_core(xh, y, core, xl, z):
    return xh, y, 1 - core, xl, z


def next_rows(step):
    def where(xh, y, core, xl, z):
        seq = xh * 8 + y * 2 + core + step
        if seq < 0 or seq > 15:
            return None
        return seq // 8, (seq // 2) % 4, seq % 2, xl, z

    return where


def shards(queries, hidden, key_weight, doc_lengths, entropy_cot):
    tokens = hidden[0]
    rows, model = tokens.shape
    half, width = key_weight.shape
    fsdp, core = lax.axis_index("xl"), lax.axis_index("core")
    seq = lax.axis_index(("xh", "y", "core"))
    place = jnp.stack([fsdp, core, seq]).astype(jnp.int32)

    quarter = model // 4
    split = rows // 2
    forward, backward = (functools.partial(along_x, step=step) for step in (1, -1))

    def column(first, last, start, count):
        return lax.dynamic_slice(tokens, (first, start), (last - first, count))

    near = [
        move(column(0, split, (1 - fsdp) * half, half), forward),
        move(column(split, rows, (1 - fsdp) * half, half), backward),
    ]
    passed = [column(0, rows, fsdp * half + (1 - core) * quarter, quarter)]
    own = column(0, rows, fsdp * half + core * quarter, quarter)
    total = project_own(place, tokens, key_weight)
    near, total, passed, own = lax.optimization_barrier((near, total, passed, own))
    low, high = project_near(*near, key_weight)
    low, high = move(low, backward), move(high, forward)
    key_own = (total + jnp.concatenate([low, high], axis=0).astype(F32)).astype(BF)
    key_halo = move(key_own, next_rows(1))

    start = (1 - core) * quarter
    passed += [lax.dynamic_slice(v, (0, start), (split, quarter)) for v in near]
    across = [move(v, swap_core) for v in passed]

    entropy, grad_query, grad_own, grad_halo = attend(
        place, doc_lengths, queries[0], key_own, key_halo, entropy_cot[0].T
    )

    grad_halo, across = lax.optimization_barrier((grad_halo, across))
    from_next = move(grad_halo, next_rows(-1))
    key_grad = (grad_own + from_next.astype(F32)).astype(BF)
    grad_near = [move(key_grad[:split], forward), move(key_grad[split:], backward)]
    grads = [key_grad, *grad_near, move(key_grad, swap_core)]
    grads += [move(v, swap_core) for v in grad_near]

    chips = ("xh", "y", "z")
    parts = weight_grad(place, own, near, across, grads).reshape(32, 64, width)
    parts = lax.all_to_all(parts, chips, split_axis=0, concat_axis=0, tiled=True)
    spread = sum_spread(parts, (rows * 16 * 8) ** (-0.5))
    final = lax.all_to_all(spread, chips, split_axis=0, concat_axis=0, tiled=True).reshape(2048, width)
    part = 1024
    others = [move(final[k:k + part], swap_core) for k in range(0, 2048, part)]
    grad_weight = write_rows(final, half, 0, 0)
    for k, other in enumerate(others):
        grad_weight = write_rows(other, half, 1, k * part, grad_weight)
    return entropy.T[None], grad_query[None], grad_weight


def solution(mesh):
    fine = Mesh(mesh.devices.reshape(2, 4, 2, 2, 4), AXES)
    seq = ("xh", "y", "core")
    both = ("xl", "z")
    return jax.shard_map(
        shards,
        mesh=fine,
        in_specs=(
            P(both, seq, None),
            P(both, seq, None),
            P("xl", None),
            P(both, None),
            P(both, seq, None),
        ),
        out_specs=(P(both, seq, None), P(both, seq, None), P("xl", None)),
        check_vma=False,
    )
```

```python
import functools
import math

import jax
import jax.numpy as jnp
from jax import lax
from jax.experimental import pallas as pl
from jax.experimental.pallas import tpu as pltpu
from jax.sharding import Mesh, PartitionSpec as P

QH = 32
KVH = 4
HD = 128
GROUP = QH // KVH
BF = jnp.bfloat16
F32 = jnp.float32
AXES = ("xh", "y", "core", "xl", "z")
FACTOR = HD ** (-0.5)
EXP_SCALE = FACTOR * math.log2(math.e)
NEG = -1e30


def coords(index):
    seq, rest = divmod(index, 8)
    fsdp, z = divmod(rest, 4)
    return seq // 8, (seq // 2) % 4, seq % 2, fsdp, z


def linear(xh, y, core, xl, z):
    return ((xh * 8 + y * 2 + core) * 2 + xl) * 4 + z


def move(value, where):
    pairs = []
    for index in range(128):
        target = where(*coords(index))
        if target is not None:
            pairs.append((index, linear(*target)))
    return lax.ppermute(value, AXES, pairs)


def along_x(xh, y, core, xl, z, step, other=0):
    x = (xh * 2 + xl + step) % 4
    return x // 2, y, core ^ other, x % 2, z


def params(mib):
    return pltpu.CompilerParams(vmem_limit_bytes=mib << 20)


def cost(flops, moved):
    return pl.CostEstimate(flops=int(flops), bytes_accessed=int(moved), transcendentals=0)


def own_half_kernel(place, hidden, weight, out):
    @pl.when(pl.program_id(0) == 0)
    def _():
        out[...] = jnp.zeros_like(out)

    out[...] += jnp.dot(hidden[...], weight[...], preferred_element_type=F32)


def project_own(place, tokens, weight):
    rows, model = tokens.shape
    half, width = weight.shape
    step = half // 4
    return pl.pallas_call(
        own_half_kernel,
        grid_spec=pltpu.PrefetchScalarGridSpec(
            num_scalar_prefetch=1,
            grid=(4,),
            in_specs=[
                pl.BlockSpec((rows, step), lambda i, p: (0, p[0] * 4 + i)),
                pl.BlockSpec((step, width), lambda i, p: (i, 0)),
            ],
            out_specs=pl.BlockSpec((rows, width), lambda i, p: (0, 0)),
        ),
        out_shape=jax.ShapeDtypeStruct((rows, width), F32),
        compiler_params=params(8),
        cost_estimate=cost(2 * rows * half * width, 6 << 20),
        name="project_own",
    )(place, tokens, weight)


def near_kernel(low, high, weight, low_out, high_out, total):
    step = weight.shape[0] // 4
    count = low.shape[0]
    total[...] = jnp.zeros_like(total)

    @pl.loop(0, 4)
    def _(k):
        part = pl.ds(pl.multiple_of(k * step, step), step)
        rows = jnp.concatenate([low[:, part], high[:, part]], axis=0)
        total[...] += jnp.dot(rows, weight[part, :], preferred_element_type=F32)

    low_out[...] = total[:count].astype(BF)
    high_out[...] = total[count:].astype(BF)


def project_near(low, high, weight):
    rows = low.shape[0]
    half, width = weight.shape
    here = pl.BlockSpec(memory_space=pltpu.VMEM)
    return pl.pallas_call(
        near_kernel,
        in_specs=[here] * 3,
        out_specs=[here] * 2,
        out_shape=[jax.ShapeDtypeStruct((rows, width), BF)] * 2,
        scratch_shapes=[pltpu.VMEM((2 * rows, width), F32)],
        compiler_params=params(12),
        cost_estimate=cost(4 * rows * half * width, 6 << 20),
        name="project_near",
    )(low, high, weight)


TILE = 64
WINDOW = 256 + TILE
STACK = 256 // TILE


def attend_kernel(place, lengths, query, key_own, key_halo, weight, entropy, grad_query, grad_own,
                  grad_halo, bias, keys, keys_t, total):
    tiles = 256 // TILE

    @pl.when(pl.program_id(0) == 0)
    def _():
        base = place[2] * 256
        position = base + lax.broadcasted_iota(jnp.int32, (8, 256), 1)

        def add(i, state):
            end, first = state
            end = end + lengths[0, i]
            return end, jnp.where(position >= end, end, first)

        _, first = lax.fori_loop(
            0, lengths.shape[1], add, (jnp.int32(0), jnp.zeros((8, 256), jnp.int32))
        )
        for tile in range(tiles):
            rows = slice(tile * TILE, (tile + 1) * TILE)
            begin = jnp.concatenate([first[0:1, rows]] * STACK, axis=1)
            here = jnp.concatenate([position[0:1, rows]] * STACK, axis=1)
            there = base - 256 + tile * TILE + lax.broadcasted_iota(jnp.int32, (WINDOW, 256), 0)
            bias[tile] = jnp.where((there >= begin) & (there <= here), 0.0, NEG)

    keys[0:256, :] = key_halo[...]
    keys[256:512, :] = key_own[...]
    keys_t[0] = keys[...].T
    keys_t[1, :, 0:512 - TILE] = keys[TILE:512, :].T
    weights = weight[...].astype(F32)
    total[...] = jnp.zeros_like(total)

    def score(group, tile):
        rows = slice(tile * TILE, (tile + 1) * TILE)
        window = slice(tile * TILE, tile * TILE + WINDOW)
        heads = range(group * STACK, (group + 1) * STACK)
        stack = jnp.concatenate([query[rows, h * HD:(h + 1) * HD] for h in heads], axis=0)
        raw = lax.dot_general(
            keys[window, :], stack, (((1,), (1,)), ((), ())), preferred_element_type=F32
        ) + bias[tile]
        return raw, stack

    def soften(group, tile, raw):
        rows = slice(tile * TILE, (tile + 1) * TILE)
        heads = range(group * STACK, (group + 1) * STACK)
        top = jnp.max(raw, axis=0, keepdims=True)
        gap = raw - top
        power = jnp.exp2(gap * EXP_SCALE)
        den = jnp.sum(power, axis=0, keepdims=True)
        mean = jnp.sum(power * gap, axis=0, keepdims=True) / den
        row_weight = jnp.concatenate([weights[h:h + 1, rows] for h in heads], axis=1)
        slope_b = row_weight * FACTOR / den
        slope_a = slope_b * mean
        level = jnp.log(den) - FACTOR * mean
        for k, h in enumerate(heads):
            entropy[h:h + 1, rows] = level[:, k * TILE:(k + 1) * TILE]
        return (power * (slope_a - slope_b * gap)).astype(BF)

    def grads(group, tile, slope, stack):
        rows = slice(tile * TILE, (tile + 1) * TILE)
        start = tile // 2 * 2 * TILE
        turned = jnp.dot(
            keys_t[tile % 2, :, start:start + WINDOW], slope, preferred_element_type=F32
        ) * FACTOR
        straight = turned.T.astype(BF)
        for k in range(STACK):
            h = group * STACK + k
            grad_query[rows, h * HD:(h + 1) * HD] = straight[k * TILE:(k + 1) * TILE]
        window = slice(tile * TILE, tile * TILE + WINDOW)
        total[window, :] += jnp.dot(slope, stack, preferred_element_type=F32)

    order = [(group, tile) for group in range(GROUP // STACK) for tile in range(tiles)]
    ahead = score(*order[0])
    last = None
    for i, at in enumerate(order):
        raw, stack = ahead
        if i + 1 < len(order):
            ahead = score(*order[i + 1])
        if last is not None:
            grads(*last)
        last = (*at, soften(*at, raw), stack)
    grads(*last)
    grad_halo[...] = (total[0:256, :] * FACTOR).astype(grad_halo.dtype)
    grad_own[...] = total[256:512, :] * FACTOR


def attend(place, lengths, queries, key_own, key_halo, weight):
    rows, width = queries.shape
    wide = GROUP * HD
    by_head = lambda j, p, l: (0, j)
    return pl.pallas_call(
        attend_kernel,
        grid_spec=pltpu.PrefetchScalarGridSpec(
            num_scalar_prefetch=2,
            grid=(KVH,),
            in_specs=[
                pl.BlockSpec((rows, wide), by_head),
                pl.BlockSpec((rows, HD), by_head),
                pl.BlockSpec((rows, HD), by_head),
                pl.BlockSpec((GROUP, rows), lambda j, p, l: (j, 0)),
            ],
            out_specs=[
                pl.BlockSpec((GROUP, rows), lambda j, p, l: (j, 0)),
                pl.BlockSpec((rows, wide), by_head),
                pl.BlockSpec((rows, HD), by_head),
                pl.BlockSpec((rows, HD), by_head),
            ],
            scratch_shapes=[
                pltpu.VMEM((256 // TILE, WINDOW, 256), F32),
                pltpu.VMEM((512, HD), BF),
                pltpu.VMEM((2, HD, 512), BF),
                pltpu.VMEM((512, HD), F32),
            ],
        ),
        out_shape=[
            jax.ShapeDtypeStruct((QH, rows), F32),
            jax.ShapeDtypeStruct((rows, width), BF),
            jax.ShapeDtypeStruct((rows, KVH * HD), F32),
            jax.ShapeDtypeStruct((rows, KVH * HD), BF),
        ],
        compiler_params=params(16),
        cost_estimate=cost(4 << 30, 6 << 20),
        name="attend",
    )(place, lengths, queries, key_own, key_halo, weight)


def weight_grad_kernel(count, far, place, *refs):
    hidden, grads, out, grad = refs[:count], refs[count:-2], refs[-2], refs[-1]
    grad[...] = jnp.concatenate([piece[...] for piece in grads], axis=0)
    step = 512

    @pl.loop(0, out.shape[0] // step)
    def _(i):
        here = pl.multiple_of(i * step, step)
        there = pl.multiple_of(place[1] * out.shape[0] + i * step, step)
        rows = jnp.concatenate(
            [piece[:, pl.ds(there if far[k] else here, step)] for k, piece in enumerate(hidden)], axis=0
        )
        total = lax.dot_general(rows, grad[...], (((0,), (0,)), ((), ())), preferred_element_type=F32)
        out[pl.ds(here, step), :] = total.astype(BF)


def weight_grad(place, own, near, swapped, grads):
    here = pl.BlockSpec(memory_space=pltpu.VMEM)
    hidden = [own, *near, *swapped]
    far = [False] + [True] * len(near) + [False] * len(swapped)
    return pl.pallas_call(
        functools.partial(weight_grad_kernel, len(hidden), far),
        in_specs=[pl.BlockSpec(memory_space=pltpu.SMEM)] + [here] * (len(hidden) + len(grads)),
        out_specs=here,
        out_shape=jax.ShapeDtypeStruct((2048, 512), BF),
        scratch_shapes=[pltpu.VMEM((1024, 512), BF)],
        compiler_params=params(16),
        cost_estimate=cost(2 * 1024 * 2048 * 512, 8 << 20),
        name="weight_grad",
    )(place, *hidden, *grads)


def sum_spread_kernel(scale, parts, out):
    total = parts[0].astype(F32)
    for k in range(1, parts.shape[0]):
        total = total + parts[k].astype(F32)
    low = (total * scale).astype(BF)
    for k in range(parts.shape[0]):
        out[k] = low


def sum_spread(parts, scale):
    count, rows, width = parts.shape
    block = pl.BlockSpec((count, rows // 4, width), lambda i: (0, i, 0))
    return pl.pallas_call(
        functools.partial(sum_spread_kernel, scale),
        grid=(4,),
        in_specs=[block],
        out_specs=block,
        out_shape=jax.ShapeDtypeStruct(parts.shape, BF),
        compiler_params=params(8),
        cost_estimate=cost(2 << 20, 4 << 20),
        name="sum_spread",
    )(parts)


def copy_kernel(side, first, rows, *refs):
    out, done = refs[-2], refs[-1]
    core = lax.axis_index("core")
    start = (1 - core if side else core) * (out.shape[0] // 2) + first
    start = pl.multiple_of(start, rows.shape[0])
    copy = pltpu.make_async_copy(rows, out.at[pl.ds(start, rows.shape[0])], done)
    copy.start()
    copy.wait()


def write_rows(rows, total, side, first, held=None):
    count, width = rows.shape
    anywhere = pl.BlockSpec(memory_space=pl.ANY)
    given = [rows] if held is None else [rows, held]
    return pl.pallas_call(
        functools.partial(copy_kernel, side, first),
        in_specs=[anywhere] * len(given),
        out_specs=anywhere,
        out_shape=jax.ShapeDtypeStruct((total, width), BF),
        scratch_shapes=[pltpu.SemaphoreType.DMA],
        input_output_aliases={} if held is None else {1: 0},
        compiler_params=params(4),
        cost_estimate=cost(1 << 20, 4 << 20),
        name="write_rows",
    )(*given)


def swap_core(xh, y, core, xl, z):
    return xh, y, 1 - core, xl, z


def next_rows(step):
    def where(xh, y, core, xl, z):
        seq = xh * 8 + y * 2 + core + step
        if seq < 0 or seq > 15:
            return None
        return seq // 8, (seq // 2) % 4, seq % 2, xl, z

    return where


def shards(queries, hidden, key_weight, doc_lengths, entropy_cot):
    tokens = hidden[0]
    rows, model = tokens.shape
    half, width = key_weight.shape
    fsdp, core = lax.axis_index("xl"), lax.axis_index("core")
    seq = lax.axis_index(("xh", "y", "core"))
    place = jnp.stack([fsdp, core, seq]).astype(jnp.int32)

    quarter = model // 4
    split = rows // 2
    forward, backward = (functools.partial(along_x, step=step) for step in (1, -1))

    def column(first, last, start, count):
        return lax.dynamic_slice(tokens, (first, start), (last - first, count))

    near = [
        move(column(0, split, (1 - fsdp) * half, half), forward),
        move(column(split, rows, (1 - fsdp) * half, half), backward),
    ]
    passed = [column(0, rows, fsdp * half + (1 - core) * quarter, quarter)]
    own = column(0, rows, fsdp * half + core * quarter, quarter)
    total = project_own(place, tokens, key_weight)
    near, total, passed, own = lax.optimization_barrier((near, total, passed, own))
    low, high = project_near(*near, key_weight)
    low, high = move(low, backward), move(high, forward)
    key_own = (total + jnp.concatenate([low, high], axis=0).astype(F32)).astype(BF)
    key_halo = move(key_own, next_rows(1))

    start = (1 - core) * quarter
    passed += [lax.dynamic_slice(v, (0, start), (split, quarter)) for v in near]
    across = [move(v, swap_core) for v in passed]

    entropy, grad_query, grad_own, grad_halo = attend(
        place, doc_lengths, queries[0], key_own, key_halo, entropy_cot[0].T
    )

    grad_halo, across = lax.optimization_barrier((grad_halo, across))
    from_next = move(grad_halo, next_rows(-1))
    key_grad = (grad_own + from_next.astype(F32)).astype(BF)
    grad_near = [move(key_grad[:split], forward), move(key_grad[split:], backward)]
    grads = [key_grad, *grad_near, move(key_grad, swap_core)]
    grads += [move(v, swap_core) for v in grad_near]

    chips = ("xh", "y", "z")
    parts = weight_grad(place, own, near, across, grads).reshape(32, 64, width)
    parts = lax.all_to_all(parts, chips, split_axis=0, concat_axis=0, tiled=True)
    spread = sum_spread(parts, (rows * 16 * 8) ** (-0.5))
    final = lax.all_to_all(spread, chips, split_axis=0, concat_axis=0, tiled=True).reshape(2048, width)
    part = 1024
    others = [move(final[k:k + part], swap_core) for k in range(0, 2048, part)]
    grad_weight = write_rows(final, half, 0, 0)
    for k, other in enumerate(others):
        grad_weight = write_rows(other, half, 1, k * part, grad_weight)
    return entropy.T[None], grad_query[None], grad_weight


def solution(mesh):
    fine = Mesh(mesh.devices.reshape(2, 4, 2, 2, 4), AXES)
    seq = ("xh", "y", "core")
    both = ("xl", "z")
    return jax.shard_map(
        shards,
        mesh=fine,
        in_specs=(
            P(both, seq, None),
            P(both, seq, None),
            P("xl", None),
            P(both, None),
            P(both, seq, None),
        ),
        out_specs=(P(both, seq, None), P(both, seq, None), P("xl", None)),
        check_vma=False,
    )
```

```python
import functools
import math

import jax
import jax.numpy as jnp
from jax import lax
from jax.experimental import pallas as pl
from jax.experimental.pallas import tpu as pltpu
from jax.sharding import Mesh, PartitionSpec as P

QH = 32
KVH = 4
HD = 128
GROUP = QH // KVH
BF = jnp.bfloat16
F32 = jnp.float32
AXES = ("xh", "y", "core", "xl", "z")
FACTOR = HD ** (-0.5)
EXP_SCALE = FACTOR * math.log2(math.e)
NEG = -1e30


def coords(index):
    seq, rest = divmod(index, 8)
    fsdp, z = divmod(rest, 4)
    return seq // 8, (seq // 2) % 4, seq % 2, fsdp, z


def linear(xh, y, core, xl, z):
    return ((xh * 8 + y * 2 + core) * 2 + xl) * 4 + z


def move(value, where):
    pairs = []
    for index in range(128):
        target = where(*coords(index))
        if target is not None:
            pairs.append((index, linear(*target)))
    return lax.ppermute(value, AXES, pairs)


def along_x(xh, y, core, xl, z, step, other=0):
    x = (xh * 2 + xl + step) % 4
    return x // 2, y, core ^ other, x % 2, z


def params(mib):
    return pltpu.CompilerParams(vmem_limit_bytes=mib << 20)


def cost(flops, moved):
    return pl.CostEstimate(flops=int(flops), bytes_accessed=int(moved), transcendentals=0)


def own_half_kernel(place, hidden, weight, out):
    @pl.when(pl.program_id(0) == 0)
    def _():
        out[...] = jnp.zeros_like(out)

    out[...] += jnp.dot(hidden[...], weight[...], preferred_element_type=F32)


def project_own(place, tokens, weight):
    rows, model = tokens.shape
    half, width = weight.shape
    step = half // 4
    return pl.pallas_call(
        own_half_kernel,
        grid_spec=pltpu.PrefetchScalarGridSpec(
            num_scalar_prefetch=1,
            grid=(4,),
            in_specs=[
                pl.BlockSpec((rows, step), lambda i, p: (0, p[0] * 4 + i)),
                pl.BlockSpec((step, width), lambda i, p: (i, 0)),
            ],
            out_specs=pl.BlockSpec((rows, width), lambda i, p: (0, 0)),
        ),
        out_shape=jax.ShapeDtypeStruct((rows, width), F32),
        compiler_params=params(8),
        cost_estimate=cost(2 * rows * half * width, 6 << 20),
        name="project_own",
    )(place, tokens, weight)


def near_kernel(low, high, weight, low_out, high_out, total):
    step = weight.shape[0] // 2
    count = low.shape[0]
    total[...] = jnp.zeros_like(total)

    @pl.loop(0, 2)
    def _(k):
        part = pl.ds(pl.multiple_of(k * step, step), step)
        rows = jnp.concatenate([low[:, part], high[:, part]], axis=0)
        total[...] += jnp.dot(rows, weight[part, :], preferred_element_type=F32)

    low_out[...] = total[:count].astype(BF)
    high_out[...] = total[count:].astype(BF)


def project_near(low, high, weight):
    rows = low.shape[0]
    half, width = weight.shape
    here = pl.BlockSpec(memory_space=pltpu.VMEM)
    return pl.pallas_call(
        near_kernel,
        in_specs=[here] * 3,
        out_specs=[here] * 2,
        out_shape=[jax.ShapeDtypeStruct((rows, width), BF)] * 2,
        scratch_shapes=[pltpu.VMEM((2 * rows, width), F32)],
        compiler_params=params(12),
        cost_estimate=cost(4 * rows * half * width, 6 << 20),
        name="project_near",
    )(low, high, weight)


TILE = 32
WINDOW = 256 + TILE
STACK = 256 // TILE


def attend_kernel(place, lengths, query, key_own, key_halo, weight, entropy, grad_query, grad_own,
                  grad_halo, bias, keys, keys_t, total):
    tiles = 256 // TILE

    @pl.when(pl.program_id(0) == 0)
    def _():
        base = place[2] * 256
        position = base + lax.broadcasted_iota(jnp.int32, (8, 256), 1)

        def add(i, state):
            end, first = state
            end = end + lengths[0, i]
            return end, jnp.where(position >= end, end, first)

        _, first = lax.fori_loop(
            0, lengths.shape[1], add, (jnp.int32(0), jnp.zeros((8, 256), jnp.int32))
        )
        for tile in range(tiles):
            rows = slice(tile * TILE, (tile + 1) * TILE)
            begin = jnp.concatenate([first[0:1, rows]] * STACK, axis=1)
            here = jnp.concatenate([position[0:1, rows]] * STACK, axis=1)
            there = base - 256 + tile * TILE + lax.broadcasted_iota(jnp.int32, (WINDOW, 256), 0)
            bias[tile] = jnp.where((there >= begin) & (there <= here), 0.0, NEG)

    keys[0:256, :] = key_halo[...]
    keys[256:512, :] = key_own[...]
    keys_t[0] = keys[...].T
    for k in range(1, 128 // TILE):
        keys_t[k, :, 0:512 - k * TILE] = keys[k * TILE:512, :].T
    weights = weight[...].astype(F32)
    total[...] = jnp.zeros_like(total)

    def score(group, tile):
        rows = slice(tile * TILE, (tile + 1) * TILE)
        window = slice(tile * TILE, tile * TILE + WINDOW)
        heads = range(group * STACK, (group + 1) * STACK)
        stack = jnp.concatenate([query[rows, h * HD:(h + 1) * HD] for h in heads], axis=0)
        raw = lax.dot_general(
            keys[window, :], stack, (((1,), (1,)), ((), ())), preferred_element_type=F32
        ) + bias[tile]
        return raw, stack

    def soften(group, tile, raw):
        rows = slice(tile * TILE, (tile + 1) * TILE)
        heads = range(group * STACK, (group + 1) * STACK)
        top = jnp.max(raw, axis=0, keepdims=True)
        gap = raw - top
        power = jnp.exp2(gap * EXP_SCALE)
        den = jnp.sum(power, axis=0, keepdims=True)
        mean = jnp.sum(power * gap, axis=0, keepdims=True) / den
        row_weight = jnp.concatenate([weights[h:h + 1, rows] for h in heads], axis=1)
        slope_b = row_weight * FACTOR / den
        slope_a = slope_b * mean
        level = jnp.log(den) - FACTOR * mean
        for k, h in enumerate(heads):
            entropy[h:h + 1, rows] = level[:, k * TILE:(k + 1) * TILE]
        return (power * (slope_a - slope_b * gap)).astype(BF)

    def grads(group, tile, slope, stack):
        rows = slice(tile * TILE, (tile + 1) * TILE)
        start = tile * TILE // 128 * 128
        turned = jnp.dot(
            keys_t[tile % (128 // TILE), :, start:start + WINDOW], slope, preferred_element_type=F32
        ) * FACTOR
        straight = turned.T.astype(BF)
        for k in range(STACK):
            h = group * STACK + k
            grad_query[rows, h * HD:(h + 1) * HD] = straight[k * TILE:(k + 1) * TILE]
        window = slice(tile * TILE, tile * TILE + WINDOW)
        total[window, :] += jnp.dot(slope, stack, preferred_element_type=F32)

    order = [(group, tile) for group in range(GROUP // STACK) for tile in range(tiles)]
    ahead = score(*order[0])
    last = None
    for i, at in enumerate(order):
        raw, stack = ahead
        if i + 1 < len(order):
            ahead = score(*order[i + 1])
        if last is not None:
            grads(*last)
        last = (*at, soften(*at, raw), stack)
    grads(*last)
    grad_halo[...] = (total[0:256, :] * FACTOR).astype(grad_halo.dtype)
    grad_own[...] = total[256:512, :] * FACTOR


def attend(place, lengths, queries, key_own, key_halo, weight):
    rows, width = queries.shape
    wide = GROUP * HD
    by_head = lambda j, p, l: (0, j)
    return pl.pallas_call(
        attend_kernel,
        grid_spec=pltpu.PrefetchScalarGridSpec(
            num_scalar_prefetch=2,
            grid=(KVH,),
            in_specs=[
                pl.BlockSpec((rows, wide), by_head),
                pl.BlockSpec((rows, HD), by_head),
                pl.BlockSpec((rows, HD), by_head),
                pl.BlockSpec((GROUP, rows), lambda j, p, l: (j, 0)),
            ],
            out_specs=[
                pl.BlockSpec((GROUP, rows), lambda j, p, l: (j, 0)),
                pl.BlockSpec((rows, wide), by_head),
                pl.BlockSpec((rows, HD), by_head),
                pl.BlockSpec((rows, HD), by_head),
            ],
            scratch_shapes=[
                pltpu.VMEM((256 // TILE, WINDOW, 256), F32),
                pltpu.VMEM((512, HD), BF),
                pltpu.VMEM((128 // TILE, HD, 512), BF),
                pltpu.VMEM((512, HD), F32),
            ],
        ),
        out_shape=[
            jax.ShapeDtypeStruct((QH, rows), F32),
            jax.ShapeDtypeStruct((rows, width), BF),
            jax.ShapeDtypeStruct((rows, KVH * HD), F32),
            jax.ShapeDtypeStruct((rows, KVH * HD), BF),
        ],
        compiler_params=params(16),
        cost_estimate=cost(4 << 30, 6 << 20),
        name="attend",
    )(place, lengths, queries, key_own, key_halo, weight)


def weight_grad_kernel(count, far, more, place, *refs):
    hidden, grads, out, grad = refs[:count], refs[count:2 * count], refs[-2], refs[-1]
    grad[...] = jnp.concatenate([piece[...] for piece in grads], axis=0)
    step = 512

    @pl.loop(0, out.shape[0] // step)
    def _(i):
        here = pl.multiple_of(i * step, step)
        there = pl.multiple_of(place[1] * out.shape[0] + i * step, step)
        rows = jnp.concatenate(
            [piece[:, pl.ds(there if far[k] else here, step)] for k, piece in enumerate(hidden)], axis=0
        )
        total = lax.dot_general(rows, grad[...], (((0,), (0,)), ((), ())), preferred_element_type=F32)
        if more:
            total = total + refs[2 * count][pl.ds(here, step), :]
        out[pl.ds(here, step), :] = total.astype(out.dtype)


def weight_grad(place, hidden, far, grads, dtype, held=None):
    here = pl.BlockSpec(memory_space=pltpu.VMEM)
    more = [] if held is None else [held]
    count = sum(v.shape[0] for v in grads)
    return pl.pallas_call(
        functools.partial(weight_grad_kernel, len(hidden), far, len(more)),
        in_specs=[pl.BlockSpec(memory_space=pltpu.SMEM)] + [here] * (2 * len(hidden) + len(more)),
        out_specs=here,
        out_shape=jax.ShapeDtypeStruct((2048, 512), dtype),
        scratch_shapes=[pltpu.VMEM((count, 512), BF)],
        compiler_params=params(16),
        cost_estimate=cost(2 * count * 2048 * 512, 8 << 20),
        name="weight_grad",
    )(place, *hidden, *grads, *more)


def sum_spread_kernel(scale, parts, out):
    total = parts[0].astype(F32)
    for k in range(1, parts.shape[0]):
        total = total + parts[k].astype(F32)
    low = (total * scale).astype(BF)
    for k in range(parts.shape[0]):
        out[k] = low


def sum_spread(parts, scale):
    count, rows, width = parts.shape
    block = pl.BlockSpec((count, rows // 4, width), lambda i: (0, i, 0))
    return pl.pallas_call(
        functools.partial(sum_spread_kernel, scale),
        grid=(4,),
        in_specs=[block],
        out_specs=block,
        out_shape=jax.ShapeDtypeStruct(parts.shape, BF),
        compiler_params=params(8),
        cost_estimate=cost(2 << 20, 4 << 20),
        name="sum_spread",
    )(parts)


def copy_kernel(side, first, rows, *refs):
    out, done = refs[-2], refs[-1]
    core = lax.axis_index("core")
    start = (1 - core if side else core) * (out.shape[0] // 2) + first
    start = pl.multiple_of(start, rows.shape[0])
    copy = pltpu.make_async_copy(rows, out.at[pl.ds(start, rows.shape[0])], done)
    copy.start()
    copy.wait()


def write_rows(rows, total, side, first, held=None):
    count, width = rows.shape
    anywhere = pl.BlockSpec(memory_space=pl.ANY)
    given = [rows] if held is None else [rows, held]
    return pl.pallas_call(
        functools.partial(copy_kernel, side, first),
        in_specs=[anywhere] * len(given),
        out_specs=anywhere,
        out_shape=jax.ShapeDtypeStruct((total, width), BF),
        scratch_shapes=[pltpu.SemaphoreType.DMA],
        input_output_aliases={} if held is None else {1: 0},
        compiler_params=params(4),
        cost_estimate=cost(1 << 20, 4 << 20),
        name="write_rows",
    )(*given)


def swap_core(xh, y, core, xl, z):
    return xh, y, 1 - core, xl, z


def next_rows(step):
    def where(xh, y, core, xl, z):
        seq = xh * 8 + y * 2 + core + step
        if seq < 0 or seq > 15:
            return None
        return seq // 8, (seq // 2) % 4, seq % 2, xl, z

    return where


def shards(queries, hidden, key_weight, doc_lengths, entropy_cot):
    tokens = hidden[0]
    rows, model = tokens.shape
    half, width = key_weight.shape
    fsdp, core = lax.axis_index("xl"), lax.axis_index("core")
    seq = lax.axis_index(("xh", "y", "core"))
    place = jnp.stack([fsdp, core, seq]).astype(jnp.int32)

    quarter = model // 4
    split = rows // 2
    forward, backward = (functools.partial(along_x, step=step) for step in (1, -1))

    def column(first, last, start, count):
        return lax.dynamic_slice(tokens, (first, start), (last - first, count))

    near = [
        move(column(0, split, (1 - fsdp) * half, half), forward),
        move(column(split, rows, (1 - fsdp) * half, half), backward),
    ]
    passed = [column(0, rows, fsdp * half + (1 - core) * quarter, quarter)]
    own = column(0, rows, fsdp * half + core * quarter, quarter)
    total = project_own(place, tokens, key_weight)
    near, total, passed, own = lax.optimization_barrier((near, total, passed, own))
    low, high = project_near(*near, key_weight)
    low, high = move(low, backward), move(high, forward)
    key_own = (total + jnp.concatenate([low, high], axis=0).astype(F32)).astype(BF)
    key_halo = move(key_own, next_rows(1))

    start = (1 - core) * quarter
    passed += [lax.dynamic_slice(v, (0, start), (split, quarter)) for v in near]
    across = [move(v, swap_core) for v in passed]

    entropy, grad_query, grad_own, grad_halo = attend(
        place, doc_lengths, queries[0], key_own, key_halo, entropy_cot[0].T
    )

    grad_halo, across = lax.optimization_barrier((grad_halo, across))
    from_next = move(grad_halo, next_rows(-1))
    key_grad = (grad_own + from_next.astype(F32)).astype(BF)
    grad_near = [move(key_grad[:split], forward), move(key_grad[split:], backward)]
    grads = [key_grad, move(key_grad, swap_core)]
    parts = weight_grad(place, [own, across[0]], [False, False], grads, F32)
    grad_near, parts = lax.optimization_barrier((grad_near, parts))
    grads = [*grad_near, *(move(v, swap_core) for v in grad_near)]
    far = [True, True, False, False]
    parts = weight_grad(place, [*near, *across[1:]], far, grads, BF, parts)

    chips = ("xh", "y", "z")
    parts = lax.all_to_all(parts.reshape(32, 64, width), chips, split_axis=0, concat_axis=0, tiled=True)
    spread = sum_spread(parts, (rows * 16 * 8) ** (-0.5))
    final = lax.all_to_all(spread, chips, split_axis=0, concat_axis=0, tiled=True).reshape(2048, width)
    part = 1024
    others = [move(final[k:k + part], swap_core) for k in range(0, 2048, part)]
    grad_weight = write_rows(final, half, 0, 0)
    for k, other in enumerate(others):
        grad_weight = write_rows(other, half, 1, k * part, grad_weight)
    return entropy.T[None], grad_query[None], grad_weight


def solution(mesh):
    fine = Mesh(mesh.devices.reshape(2, 4, 2, 2, 4), AXES)
    seq = ("xh", "y", "core")
    both = ("xl", "z")
    return jax.shard_map(
        shards,
        mesh=fine,
        in_specs=(
            P(both, seq, None),
            P(both, seq, None),
            P("xl", None),
            P(both, None),
            P(both, seq, None),
        ),
        out_specs=(P(both, seq, None), P(both, seq, None), P("xl", None)),
        check_vma=False,
    )
```

```python
import functools
import math

import jax
import jax.numpy as jnp
from jax import lax
from jax.experimental import pallas as pl
from jax.experimental.pallas import tpu as pltpu
from jax.sharding import Mesh, PartitionSpec as P

QH = 32
KVH = 4
HD = 128
GROUP = QH // KVH
BF = jnp.bfloat16
F32 = jnp.float32
AXES = ("xh", "y", "core", "xl", "z")
FACTOR = HD ** (-0.5)
EXP_SCALE = FACTOR * math.log2(math.e)
NEG = -1e30


def coords(index):
    seq, rest = divmod(index, 8)
    fsdp, z = divmod(rest, 4)
    return seq // 8, (seq // 2) % 4, seq % 2, fsdp, z


def linear(xh, y, core, xl, z):
    return ((xh * 8 + y * 2 + core) * 2 + xl) * 4 + z


def move(value, where):
    pairs = []
    for index in range(128):
        target = where(*coords(index))
        if target is not None:
            pairs.append((index, linear(*target)))
    return lax.ppermute(value, AXES, pairs)


def along_x(xh, y, core, xl, z, step, other=0):
    x = (xh * 2 + xl + step) % 4
    return x // 2, y, core ^ other, x % 2, z


def params(mib):
    return pltpu.CompilerParams(vmem_limit_bytes=mib << 20)


def cost(flops, moved):
    return pl.CostEstimate(flops=int(flops), bytes_accessed=int(moved), transcendentals=0)


def own_half_kernel(place, hidden, weight, out):
    @pl.when(pl.program_id(0) == 0)
    def _():
        out[...] = jnp.zeros_like(out)

    out[...] += jnp.dot(hidden[...], weight[...], preferred_element_type=F32)


def project_own(place, tokens, weight):
    rows, model = tokens.shape
    half, width = weight.shape
    step = half // 4
    return pl.pallas_call(
        own_half_kernel,
        grid_spec=pltpu.PrefetchScalarGridSpec(
            num_scalar_prefetch=1,
            grid=(4,),
            in_specs=[
                pl.BlockSpec((rows, step), lambda i, p: (0, p[0] * 4 + i)),
                pl.BlockSpec((step, width), lambda i, p: (i, 0)),
            ],
            out_specs=pl.BlockSpec((rows, width), lambda i, p: (0, 0)),
        ),
        out_shape=jax.ShapeDtypeStruct((rows, width), F32),
        compiler_params=params(8),
        cost_estimate=cost(2 * rows * half * width, 6 << 20),
        name="project_own",
    )(place, tokens, weight)


def near_kernel(low, high, weight, low_out, high_out, total):
    step = weight.shape[0] // 2
    count = low.shape[0]
    total[...] = jnp.zeros_like(total)

    @pl.loop(0, 2)
    def _(k):
        part = pl.ds(pl.multiple_of(k * step, step), step)
        rows = jnp.concatenate([low[:, part], high[:, part]], axis=0)
        total[...] += jnp.dot(rows, weight[part, :], preferred_element_type=F32)

    low_out[...] = total[:count].astype(BF)
    high_out[...] = total[count:].astype(BF)


def project_near(low, high, weight):
    rows = low.shape[0]
    half, width = weight.shape
    here = pl.BlockSpec(memory_space=pltpu.VMEM)
    return pl.pallas_call(
        near_kernel,
        in_specs=[here] * 3,
        out_specs=[here] * 2,
        out_shape=[jax.ShapeDtypeStruct((rows, width), BF)] * 2,
        scratch_shapes=[pltpu.VMEM((2 * rows, width), F32)],
        compiler_params=params(12),
        cost_estimate=cost(4 * rows * half * width, 6 << 20),
        name="project_near",
    )(low, high, weight)


TILE = 32
WINDOW = 256 + TILE
STACK = 256 // TILE


def attend_kernel(place, lengths, query, key_own, key_halo, weight, entropy, grad_query, grad_own,
                  grad_halo, bias, keys, keys_t, total):
    tiles = 256 // TILE

    @pl.when(pl.program_id(0) == 0)
    def _():
        base = place[2] * 256
        position = base + lax.broadcasted_iota(jnp.int32, (8, 256), 1)

        def add(i, state):
            end, first = state
            end = end + lengths[0, i]
            return end, jnp.where(position >= end, end, first)

        _, first = lax.fori_loop(
            0, lengths.shape[1], add, (jnp.int32(0), jnp.zeros((8, 256), jnp.int32))
        )
        for tile in range(tiles):
            rows = slice(tile * TILE, (tile + 1) * TILE)
            begin = jnp.concatenate([first[0:1, rows]] * STACK, axis=1)
            here = jnp.concatenate([position[0:1, rows]] * STACK, axis=1)
            there = base - 256 + tile * TILE + lax.broadcasted_iota(jnp.int32, (WINDOW, 256), 0)
            bias[tile] = jnp.where((there >= begin) & (there <= here), 0.0, NEG)

    keys[0:256, :] = key_halo[...]
    keys[256:512, :] = key_own[...]
    keys_t[0] = keys[...].T
    for k in range(1, 128 // TILE):
        keys_t[k, :, 0:512 - k * TILE] = keys[k * TILE:512, :].T
    weights = weight[...].astype(F32)
    total[...] = jnp.zeros_like(total)

    def score(group, tile):
        rows = slice(tile * TILE, (tile + 1) * TILE)
        window = slice(tile * TILE, tile * TILE + WINDOW)
        heads = range(group * STACK, (group + 1) * STACK)
        stack = jnp.concatenate([query[rows, h * HD:(h + 1) * HD] for h in heads], axis=0)
        raw = lax.dot_general(
            keys[window, :], stack, (((1,), (1,)), ((), ())), preferred_element_type=F32
        ) + bias[tile]
        return raw, stack

    def soften(group, tile, raw):
        rows = slice(tile * TILE, (tile + 1) * TILE)
        heads = range(group * STACK, (group + 1) * STACK)
        top = jnp.max(raw, axis=0, keepdims=True)
        gap = raw - top
        power = jnp.exp2(gap * EXP_SCALE)
        den = jnp.sum(power, axis=0, keepdims=True)
        mean = jnp.sum(power * gap, axis=0, keepdims=True) / den
        row_weight = jnp.concatenate([weights[h:h + 1, rows] for h in heads], axis=1)
        slope_b = row_weight * FACTOR / den
        slope_a = slope_b * mean
        level = jnp.log(den) - FACTOR * mean
        for k, h in enumerate(heads):
            entropy[h:h + 1, rows] = level[:, k * TILE:(k + 1) * TILE]
        return (power * (slope_a - slope_b * gap)).astype(BF)

    def grads(group, tile, slope, stack):
        rows = slice(tile * TILE, (tile + 1) * TILE)
        start = tile * TILE // 128 * 128
        turned = jnp.dot(
            keys_t[tile % (128 // TILE), :, start:start + WINDOW], slope, preferred_element_type=F32
        ) * FACTOR
        straight = turned.T.astype(BF)
        for k in range(STACK):
            h = group * STACK + k
            grad_query[rows, h * HD:(h + 1) * HD] = straight[k * TILE:(k + 1) * TILE]
        window = slice(tile * TILE, tile * TILE + WINDOW)
        total[window, :] += jnp.dot(slope, stack, preferred_element_type=F32)

    order = [(group, tile) for group in range(GROUP // STACK) for tile in range(tiles)]
    ahead = score(*order[0])
    last = None
    for i, at in enumerate(order):
        raw, stack = ahead
        if i + 1 < len(order):
            ahead = score(*order[i + 1])
        if last is not None:
            grads(*last)
        last = (*at, soften(*at, raw), stack)
    grads(*last)
    grad_halo[...] = (total[0:256, :] * FACTOR).astype(grad_halo.dtype)
    grad_own[...] = total[256:512, :] * FACTOR


def attend(place, lengths, queries, key_own, key_halo, weight):
    rows, width = queries.shape
    wide = GROUP * HD
    by_head = lambda j, p, l: (0, j)
    return pl.pallas_call(
        attend_kernel,
        grid_spec=pltpu.PrefetchScalarGridSpec(
            num_scalar_prefetch=2,
            grid=(KVH,),
            in_specs=[
                pl.BlockSpec((rows, wide), by_head),
                pl.BlockSpec((rows, HD), by_head),
                pl.BlockSpec((rows, HD), by_head),
                pl.BlockSpec((GROUP, rows), lambda j, p, l: (j, 0)),
            ],
            out_specs=[
                pl.BlockSpec((GROUP, rows), lambda j, p, l: (j, 0)),
                pl.BlockSpec((rows, wide), by_head),
                pl.BlockSpec((rows, HD), by_head),
                pl.BlockSpec((rows, HD), by_head),
            ],
            scratch_shapes=[
                pltpu.VMEM((256 // TILE, WINDOW, 256), F32),
                pltpu.VMEM((512, HD), BF),
                pltpu.VMEM((128 // TILE, HD, 512), BF),
                pltpu.VMEM((512, HD), F32),
            ],
        ),
        out_shape=[
            jax.ShapeDtypeStruct((QH, rows), F32),
            jax.ShapeDtypeStruct((rows, width), BF),
            jax.ShapeDtypeStruct((rows, KVH * HD), F32),
            jax.ShapeDtypeStruct((rows, KVH * HD), BF),
        ],
        compiler_params=params(16),
        cost_estimate=cost(4 << 30, 6 << 20),
        name="attend",
    )(place, lengths, queries, key_own, key_halo, weight)


def weight_grad_kernel(count, far, more, place, *refs):
    hidden, grads, out, grad = refs[:count], refs[count:2 * count], refs[-2], refs[-1]
    grad[...] = jnp.concatenate([piece[...] for piece in grads], axis=0)
    step = 1024

    @pl.loop(0, out.shape[0] // step)
    def _(i):
        here = pl.multiple_of(i * step, step)
        there = pl.multiple_of(place[1] * out.shape[0] + i * step, step)
        rows = jnp.concatenate(
            [piece[:, pl.ds(there if far[k] else here, step)] for k, piece in enumerate(hidden)], axis=0
        )
        total = lax.dot_general(rows, grad[...], (((0,), (0,)), ((), ())), preferred_element_type=F32)
        if more:
            total = total + refs[2 * count][pl.ds(here, step), :]
        out[pl.ds(here, step), :] = total.astype(out.dtype)


def weight_grad(place, hidden, far, grads, dtype, held=None):
    here = pl.BlockSpec(memory_space=pltpu.VMEM)
    more = [] if held is None else [held]
    count = sum(v.shape[0] for v in grads)
    return pl.pallas_call(
        functools.partial(weight_grad_kernel, len(hidden), far, len(more)),
        in_specs=[pl.BlockSpec(memory_space=pltpu.SMEM)] + [here] * (2 * len(hidden) + len(more)),
        out_specs=here,
        out_shape=jax.ShapeDtypeStruct((2048, 512), dtype),
        scratch_shapes=[pltpu.VMEM((count, 512), BF)],
        compiler_params=params(16),
        cost_estimate=cost(2 * count * 2048 * 512, 8 << 20),
        name="weight_grad",
    )(place, *hidden, *grads, *more)


def sum_spread_kernel(scale, parts, out):
    total = parts[0].astype(F32)
    for k in range(1, parts.shape[0]):
        total = total + parts[k].astype(F32)
    low = (total * scale).astype(BF)
    for k in range(parts.shape[0]):
        out[k] = low


def sum_spread(parts, scale):
    count, rows, width = parts.shape
    block = pl.BlockSpec((count, rows // 4, width), lambda i: (0, i, 0))
    return pl.pallas_call(
        functools.partial(sum_spread_kernel, scale),
        grid=(4,),
        in_specs=[block],
        out_specs=block,
        out_shape=jax.ShapeDtypeStruct(parts.shape, BF),
        compiler_params=params(8),
        cost_estimate=cost(2 << 20, 4 << 20),
        name="sum_spread",
    )(parts)


def copy_kernel(side, first, rows, *refs):
    out, done = refs[-2], refs[-1]
    core = lax.axis_index("core")
    start = (1 - core if side else core) * (out.shape[0] // 2) + first
    start = pl.multiple_of(start, rows.shape[0])
    copy = pltpu.make_async_copy(rows, out.at[pl.ds(start, rows.shape[0])], done)
    copy.start()
    copy.wait()


def write_rows(rows, total, side, first, held=None):
    count, width = rows.shape
    anywhere = pl.BlockSpec(memory_space=pl.ANY)
    given = [rows] if held is None else [rows, held]
    return pl.pallas_call(
        functools.partial(copy_kernel, side, first),
        in_specs=[anywhere] * len(given),
        out_specs=anywhere,
        out_shape=jax.ShapeDtypeStruct((total, width), BF),
        scratch_shapes=[pltpu.SemaphoreType.DMA],
        input_output_aliases={} if held is None else {1: 0},
        compiler_params=params(4),
        cost_estimate=cost(1 << 20, 4 << 20),
        name="write_rows",
    )(*given)


def swap_core(xh, y, core, xl, z):
    return xh, y, 1 - core, xl, z


def next_rows(step):
    def where(xh, y, core, xl, z):
        seq = xh * 8 + y * 2 + core + step
        if seq < 0 or seq > 15:
            return None
        return seq // 8, (seq // 2) % 4, seq % 2, xl, z

    return where


def shards(queries, hidden, key_weight, doc_lengths, entropy_cot):
    tokens = hidden[0]
    rows, model = tokens.shape
    half, width = key_weight.shape
    fsdp, core = lax.axis_index("xl"), lax.axis_index("core")
    seq = lax.axis_index(("xh", "y", "core"))
    place = jnp.stack([fsdp, core, seq]).astype(jnp.int32)

    quarter = model // 4
    split = rows // 2
    forward, backward = (functools.partial(along_x, step=step) for step in (1, -1))

    def column(first, last, start, count):
        return lax.dynamic_slice(tokens, (first, start), (last - first, count))

    near = [
        move(column(0, split, (1 - fsdp) * half, half), forward),
        move(column(split, rows, (1 - fsdp) * half, half), backward),
    ]
    passed = [column(0, rows, fsdp * half + (1 - core) * quarter, quarter)]
    own = column(0, rows, fsdp * half + core * quarter, quarter)
    total = project_own(place, tokens, key_weight)
    near, total, passed, own = lax.optimization_barrier((near, total, passed, own))
    low, high = project_near(*near, key_weight)
    low, high = move(low, backward), move(high, forward)
    key_own = (total + jnp.concatenate([low, high], axis=0).astype(F32)).astype(BF)
    key_halo = move(key_own, next_rows(1))

    start = (1 - core) * quarter
    passed += [lax.dynamic_slice(v, (0, start), (split, quarter)) for v in near]
    across = [move(v, swap_core) for v in passed]

    entropy, grad_query, grad_own, grad_halo = attend(
        place, doc_lengths, queries[0], key_own, key_halo, entropy_cot[0].T
    )

    grad_halo, across = lax.optimization_barrier((grad_halo, across))
    from_next = move(grad_halo, next_rows(-1))
    key_grad = (grad_own + from_next.astype(F32)).astype(BF)
    grad_near = [move(key_grad[:split], forward), move(key_grad[split:], backward)]
    grads = [key_grad, move(key_grad, swap_core)]
    parts = weight_grad(place, [own, across[0]], [False, False], grads, F32)
    grad_near, parts = lax.optimization_barrier((grad_near, parts))
    grads = [*grad_near, *(move(v, swap_core) for v in grad_near)]
    far = [True, True, False, False]
    parts = weight_grad(place, [*near, *across[1:]], far, grads, BF, parts)

    chips = ("xh", "y", "z")
    parts = lax.all_to_all(parts.reshape(32, 64, width), chips, split_axis=0, concat_axis=0, tiled=True)
    spread = sum_spread(parts, (rows * 16 * 8) ** (-0.5))
    final = lax.all_to_all(spread, chips, split_axis=0, concat_axis=0, tiled=True).reshape(2048, width)
    part = 1024
    others = [move(final[k:k + part], swap_core) for k in range(0, 2048, part)]
    grad_weight = write_rows(final, half, 0, 0)
    for k, other in enumerate(others):
        grad_weight = write_rows(other, half, 1, k * part, grad_weight)
    return entropy.T[None], grad_query[None], grad_weight


def solution(mesh):
    fine = Mesh(mesh.devices.reshape(2, 4, 2, 2, 4), AXES)
    seq = ("xh", "y", "core")
    both = ("xl", "z")
    return jax.shard_map(
        shards,
        mesh=fine,
        in_specs=(
            P(both, seq, None),
            P(both, seq, None),
            P("xl", None),
            P(both, None),
            P(both, seq, None),
        ),
        out_specs=(P(both, seq, None), P(both, seq, None), P("xl", None)),
        check_vma=False,
    )
```

```python
import functools
import math

import jax
import jax.numpy as jnp
from jax import lax
from jax.experimental import pallas as pl
from jax.experimental.pallas import tpu as pltpu
from jax.sharding import Mesh, PartitionSpec as P

QH = 32
KVH = 4
HD = 128
GROUP = QH // KVH
BF = jnp.bfloat16
F32 = jnp.float32
AXES = ("xh", "y", "core", "xl", "z")
FACTOR = HD ** (-0.5)
EXP_SCALE = FACTOR * math.log2(math.e)
NEG = -1e30


def coords(index):
    seq, rest = divmod(index, 8)
    fsdp, z = divmod(rest, 4)
    return seq // 8, (seq // 2) % 4, seq % 2, fsdp, z


def linear(xh, y, core, xl, z):
    return ((xh * 8 + y * 2 + core) * 2 + xl) * 4 + z


def move(value, where):
    pairs = []
    for index in range(128):
        target = where(*coords(index))
        if target is not None:
            pairs.append((index, linear(*target)))
    return lax.ppermute(value, AXES, pairs)


def along_x(xh, y, core, xl, z, step, other=0):
    x = (xh * 2 + xl + step) % 4
    return x // 2, y, core ^ other, x % 2, z


def params(mib):
    return pltpu.CompilerParams(vmem_limit_bytes=mib << 20)


def cost(flops, moved):
    return pl.CostEstimate(flops=int(flops), bytes_accessed=int(moved), transcendentals=0)


def own_half_kernel(place, hidden, weight, out):
    @pl.when(pl.program_id(0) == 0)
    def _():
        out[...] = jnp.zeros_like(out)

    out[...] += jnp.dot(hidden[...], weight[...], preferred_element_type=F32)


def project_own(place, tokens, weight):
    rows, model = tokens.shape
    half, width = weight.shape
    step = half // 4
    return pl.pallas_call(
        own_half_kernel,
        grid_spec=pltpu.PrefetchScalarGridSpec(
            num_scalar_prefetch=1,
            grid=(4,),
            in_specs=[
                pl.BlockSpec((rows, step), lambda i, p: (0, p[0] * 4 + i)),
                pl.BlockSpec((step, width), lambda i, p: (i, 0)),
            ],
            out_specs=pl.BlockSpec((rows, width), lambda i, p: (0, 0)),
        ),
        out_shape=jax.ShapeDtypeStruct((rows, width), F32),
        compiler_params=params(8),
        cost_estimate=cost(2 * rows * half * width, 6 << 20),
        name="project_own",
    )(place, tokens, weight)


def near_kernel(low, high, weight, low_out, high_out, total):
    step = weight.shape[0] // 2
    count = low.shape[0]
    total[...] = jnp.zeros_like(total)

    @pl.loop(0, 2)
    def _(k):
        part = pl.ds(pl.multiple_of(k * step, step), step)
        rows = jnp.concatenate([low[:, part], high[:, part]], axis=0)
        total[...] += jnp.dot(rows, weight[part, :], preferred_element_type=F32)

    low_out[...] = total[:count].astype(BF)
    high_out[...] = total[count:].astype(BF)


def project_near(low, high, weight):
    rows = low.shape[0]
    half, width = weight.shape
    here = pl.BlockSpec(memory_space=pltpu.VMEM)
    return pl.pallas_call(
        near_kernel,
        in_specs=[here] * 3,
        out_specs=[here] * 2,
        out_shape=[jax.ShapeDtypeStruct((rows, width), BF)] * 2,
        scratch_shapes=[pltpu.VMEM((2 * rows, width), F32)],
        compiler_params=params(12),
        cost_estimate=cost(4 * rows * half * width, 6 << 20),
        name="project_near",
    )(low, high, weight)


TILE = 32
WINDOW = 256 + TILE
STACK = 256 // TILE


def attend_kernel(place, lengths, query, key_own, key_halo, weight, entropy, grad_query, grad_own,
                  grad_halo, bias, keys, keys_t, total):
    tiles = 256 // TILE

    @pl.when(pl.program_id(0) == 0)
    def _():
        base = place[2] * 256
        position = base + lax.broadcasted_iota(jnp.int32, (8, 256), 1)

        def add(i, state):
            end, first = state
            end = end + lengths[0, i]
            return end, jnp.where(position >= end, end, first)

        _, first = lax.fori_loop(
            0, lengths.shape[1], add, (jnp.int32(0), jnp.zeros((8, 256), jnp.int32))
        )
        for tile in range(tiles):
            rows = slice(tile * TILE, (tile + 1) * TILE)
            begin = jnp.concatenate([first[0:1, rows]] * STACK, axis=1)
            here = jnp.concatenate([position[0:1, rows]] * STACK, axis=1)
            there = base - 256 + tile * TILE + lax.broadcasted_iota(jnp.int32, (WINDOW, 256), 0)
            bias[tile] = jnp.where((there >= begin) & (there <= here), 0.0, NEG)

    keys[0:256, :] = key_halo[...]
    keys[256:512, :] = key_own[...]
    keys_t[0] = keys[...].T
    for k in range(1, 128 // TILE):
        keys_t[k, :, 0:512 - k * TILE] = keys[k * TILE:512, :].T
    weights = weight[...].astype(F32)
    total[...] = jnp.zeros_like(total)

    def score(group, tile):
        rows = slice(tile * TILE, (tile + 1) * TILE)
        window = slice(tile * TILE, tile * TILE + WINDOW)
        heads = range(group * STACK, (group + 1) * STACK)
        stack = jnp.concatenate([query[rows, h * HD:(h + 1) * HD] for h in heads], axis=0)
        raw = lax.dot_general(
            keys[window, :], stack, (((1,), (1,)), ((), ())), preferred_element_type=F32
        ) + bias[tile]
        return raw, stack

    def soften(group, tile, raw):
        rows = slice(tile * TILE, (tile + 1) * TILE)
        heads = range(group * STACK, (group + 1) * STACK)
        top = jnp.max(raw, axis=0, keepdims=True)
        gap = raw - top
        power = jnp.exp2(gap * EXP_SCALE)
        den = jnp.sum(power, axis=0, keepdims=True)
        mean = jnp.sum(power * gap, axis=0, keepdims=True) / den
        row_weight = jnp.concatenate([weights[h:h + 1, rows] for h in heads], axis=1)
        slope_b = row_weight * FACTOR / den
        slope_a = slope_b * mean
        level = jnp.log(den) - FACTOR * mean
        for k, h in enumerate(heads):
            entropy[h:h + 1, rows] = level[:, k * TILE:(k + 1) * TILE]
        return (power * (slope_a - slope_b * gap)).astype(BF)

    def grads(group, tile, slope, stack):
        rows = slice(tile * TILE, (tile + 1) * TILE)
        start = tile * TILE // 128 * 128
        turned = jnp.dot(
            keys_t[tile % (128 // TILE), :, start:start + WINDOW], slope, preferred_element_type=F32
        ) * FACTOR
        straight = turned.T.astype(BF)
        for k in range(STACK):
            h = group * STACK + k
            grad_query[rows, h * HD:(h + 1) * HD] = straight[k * TILE:(k + 1) * TILE]
        window = slice(tile * TILE, tile * TILE + WINDOW)
        total[window, :] += jnp.dot(slope, stack, preferred_element_type=F32)

    order = [(group, tile) for group in range(GROUP // STACK) for tile in range(tiles)]
    ahead = score(*order[0])
    last = None
    for i, at in enumerate(order):
        raw, stack = ahead
        if i + 1 < len(order):
            ahead = score(*order[i + 1])
        if last is not None:
            grads(*last)
        last = (*at, soften(*at, raw), stack)
    grads(*last)
    grad_halo[...] = (total[0:256, :] * FACTOR).astype(grad_halo.dtype)
    grad_own[...] = total[256:512, :] * FACTOR


def attend(place, lengths, queries, key_own, key_halo, weight):
    rows, width = queries.shape
    wide = GROUP * HD
    by_head = lambda j, p, l: (0, j)
    return pl.pallas_call(
        attend_kernel,
        grid_spec=pltpu.PrefetchScalarGridSpec(
            num_scalar_prefetch=2,
            grid=(KVH,),
            in_specs=[
                pl.BlockSpec((rows, wide), by_head),
                pl.BlockSpec((rows, HD), by_head),
                pl.BlockSpec((rows, HD), by_head),
                pl.BlockSpec((GROUP, rows), lambda j, p, l: (j, 0)),
            ],
            out_specs=[
                pl.BlockSpec((GROUP, rows), lambda j, p, l: (j, 0)),
                pl.BlockSpec((rows, wide), by_head),
                pl.BlockSpec((rows, HD), by_head),
                pl.BlockSpec((rows, HD), by_head),
            ],
            scratch_shapes=[
                pltpu.VMEM((256 // TILE, WINDOW, 256), F32),
                pltpu.VMEM((512, HD), BF),
                pltpu.VMEM((128 // TILE, HD, 512), BF),
                pltpu.VMEM((512, HD), F32),
            ],
        ),
        out_shape=[
            jax.ShapeDtypeStruct((QH, rows), F32),
            jax.ShapeDtypeStruct((rows, width), BF),
            jax.ShapeDtypeStruct((rows, KVH * HD), F32),
            jax.ShapeDtypeStruct((rows, KVH * HD), BF),
        ],
        compiler_params=params(16),
        cost_estimate=cost(4 << 30, 6 << 20),
        name="attend",
    )(place, lengths, queries, key_own, key_halo, weight)


def weight_grad_kernel(count, far, more, place, *refs):
    hidden, grads, out, grad = refs[:count], refs[count:2 * count], refs[-2], refs[-1]
    grad[...] = jnp.concatenate([piece[...] for piece in grads], axis=0)
    step = 1024

    @pl.loop(0, out.shape[0] // step)
    def _(i):
        here = pl.multiple_of(i * step, step)
        there = pl.multiple_of(place[1] * out.shape[0] + i * step, step)
        rows = jnp.concatenate(
            [piece[:, pl.ds(there if far[k] else here, step)] for k, piece in enumerate(hidden)], axis=0
        )
        total = lax.dot_general(rows, grad[...], (((0,), (0,)), ((), ())), preferred_element_type=F32)
        if more:
            total = total + refs[2 * count][pl.ds(here, step), :]
        out[pl.ds(here, step), :] = total.astype(out.dtype)


def weight_grad(place, hidden, far, grads, dtype, held=None):
    here = pl.BlockSpec(memory_space=pltpu.VMEM)
    more = [] if held is None else [held]
    count = sum(v.shape[0] for v in grads)
    return pl.pallas_call(
        functools.partial(weight_grad_kernel, len(hidden), far, len(more)),
        in_specs=[pl.BlockSpec(memory_space=pltpu.SMEM)] + [here] * (2 * len(hidden) + len(more)),
        out_specs=here,
        out_shape=jax.ShapeDtypeStruct((2048, 512), dtype),
        scratch_shapes=[pltpu.VMEM((count, 512), BF)],
        compiler_params=params(16),
        cost_estimate=cost(2 * count * 2048 * 512, 8 << 20),
        name="weight_grad",
    )(place, *hidden, *grads, *more)


def sum_spread_kernel(scale, parts, out):
    total = parts[0].astype(F32)
    for k in range(1, parts.shape[0]):
        total = total + parts[k].astype(F32)
    low = (total * scale).astype(BF)
    for k in range(parts.shape[0]):
        out[k] = low


def sum_spread(parts, scale):
    count, rows, width = parts.shape
    block = pl.BlockSpec((count, rows // 2, width), lambda i: (0, i, 0))
    return pl.pallas_call(
        functools.partial(sum_spread_kernel, scale),
        grid=(2,),
        in_specs=[block],
        out_specs=block,
        out_shape=jax.ShapeDtypeStruct(parts.shape, BF),
        compiler_params=params(8),
        cost_estimate=cost(2 << 20, 4 << 20),
        name="sum_spread",
    )(parts)


def copy_kernel(side, first, rows, *refs):
    out, done = refs[-2], refs[-1]
    core = lax.axis_index("core")
    start = (1 - core if side else core) * (out.shape[0] // 2) + first
    start = pl.multiple_of(start, rows.shape[0])
    copy = pltpu.make_async_copy(rows, out.at[pl.ds(start, rows.shape[0])], done)
    copy.start()
    copy.wait()


def write_rows(rows, total, side, first, held=None):
    count, width = rows.shape
    anywhere = pl.BlockSpec(memory_space=pl.ANY)
    given = [rows] if held is None else [rows, held]
    return pl.pallas_call(
        functools.partial(copy_kernel, side, first),
        in_specs=[anywhere] * len(given),
        out_specs=anywhere,
        out_shape=jax.ShapeDtypeStruct((total, width), BF),
        scratch_shapes=[pltpu.SemaphoreType.DMA],
        input_output_aliases={} if held is None else {1: 0},
        compiler_params=params(4),
        cost_estimate=cost(1 << 20, 4 << 20),
        name="write_rows",
    )(*given)


def swap_core(xh, y, core, xl, z):
    return xh, y, 1 - core, xl, z


def next_rows(step):
    def where(xh, y, core, xl, z):
        seq = xh * 8 + y * 2 + core + step
        if seq < 0 or seq > 15:
            return None
        return seq // 8, (seq // 2) % 4, seq % 2, xl, z

    return where


def shards(queries, hidden, key_weight, doc_lengths, entropy_cot):
    tokens = hidden[0]
    rows, model = tokens.shape
    half, width = key_weight.shape
    fsdp, core = lax.axis_index("xl"), lax.axis_index("core")
    seq = lax.axis_index(("xh", "y", "core"))
    place = jnp.stack([fsdp, core, seq]).astype(jnp.int32)

    quarter = model // 4
    split = rows // 2
    forward, backward = (functools.partial(along_x, step=step) for step in (1, -1))

    def column(first, last, start, count):
        return lax.dynamic_slice(tokens, (first, start), (last - first, count))

    near = [
        move(column(0, split, (1 - fsdp) * half, half), forward),
        move(column(split, rows, (1 - fsdp) * half, half), backward),
    ]
    passed = [column(0, rows, fsdp * half + (1 - core) * quarter, quarter)]
    own = column(0, rows, fsdp * half + core * quarter, quarter)
    total = project_own(place, tokens, key_weight)
    near, total, passed, own = lax.optimization_barrier((near, total, passed, own))
    low, high = project_near(*near, key_weight)
    low, high = move(low, backward), move(high, forward)
    key_own = (total + jnp.concatenate([low, high], axis=0).astype(F32)).astype(BF)
    key_halo = move(key_own, next_rows(1))

    start = (1 - core) * quarter
    passed += [lax.dynamic_slice(v, (0, start), (split, quarter)) for v in near]
    across = [move(v, swap_core) for v in passed]

    entropy, grad_query, grad_own, grad_halo = attend(
        place, doc_lengths, queries[0], key_own, key_halo, entropy_cot[0].T
    )

    grad_halo, across = lax.optimization_barrier((grad_halo, across))
    from_next = move(grad_halo, next_rows(-1))
    key_grad = (grad_own + from_next.astype(F32)).astype(BF)
    grad_near = [move(key_grad[:split], forward), move(key_grad[split:], backward)]
    grads = [key_grad, move(key_grad, swap_core)]
    parts = weight_grad(place, [own, across[0]], [False, False], grads, F32)
    grad_near, parts = lax.optimization_barrier((grad_near, parts))
    grads = [*grad_near, *(move(v, swap_core) for v in grad_near)]
    far = [True, True, False, False]
    parts = weight_grad(place, [*near, *across[1:]], far, grads, BF, parts)

    chips = ("xh", "y", "z")
    parts = lax.all_to_all(parts.reshape(32, 64, width), chips, split_axis=0, concat_axis=0, tiled=True)
    spread = sum_spread(parts, (rows * 16 * 8) ** (-0.5))
    final = lax.all_to_all(spread, chips, split_axis=0, concat_axis=0, tiled=True).reshape(2048, width)
    part = 1024
    others = [move(final[k:k + part], swap_core) for k in range(0, 2048, part)]
    grad_weight = write_rows(final, half, 0, 0)
    for k, other in enumerate(others):
        grad_weight = write_rows(other, half, 1, k * part, grad_weight)
    return entropy.T[None], grad_query[None], grad_weight


def solution(mesh):
    fine = Mesh(mesh.devices.reshape(2, 4, 2, 2, 4), AXES)
    seq = ("xh", "y", "core")
    both = ("xl", "z")
    return jax.shard_map(
        shards,
        mesh=fine,
        in_specs=(
            P(both, seq, None),
            P(both, seq, None),
            P("xl", None),
            P(both, None),
            P(both, seq, None),
        ),
        out_specs=(P(both, seq, None), P(both, seq, None), P("xl", None)),
        check_vma=False,
    )
```
